256 devices in a mesh: ctx: 32 (over y_lo, z, core), head: 8 (over y_hi, x).
Axes of the slice: x: 4, y: 4 (y_hi: 2, y_lo: 2; y = y_hi * 2 + y_lo), z: 8, core: 2. Of those that a mesh axis runs over, the one named last changes fastest.
Arguments:
- fine_query: bfloat16 [8192, 4096], P('ctx', 'head'), may hold values from -181 to 181
- fine_memory: bfloat16 [2, 8192, 1024], P(None, 'ctx', 'head'), may hold values from -6.5 to 6.5
- coarse_query: bfloat16 [4096, 4096], P('ctx', 'head'), may hold values from -181 to 181
- coarse_memory: bfloat16 [2, 4096, 1024], P(None, 'ctx', 'head'), may hold values from -6.5 to 6.5
- coarse_scale: int32 [4096], P('ctx'), may hold values from 0 to 7, never falling along the last dimension, each value on 1 to 1024 neighbouring positions
- out_weight: bfloat16 [4096, 4096], P('head'), may hold values from -0.09375 to 0.09375
Outputs:
- fine_mixed: bfloat16 [8192, 4096], P(('ctx', 'head'))
- coarse_mixed: bfloat16 [4096, 4096], P(('ctx', 'head'))
The draws below stay inside these ranges and needn't reach their ends.
Inputs may be any that keep to these rules, and one draw needn't show every extreme that they name: `coarse_scale`: never falls along the coarse tokens.
All inputs are finite; a program needn't handle non-finite values.
Results may differ from the reference program's by a relative error of at most 0.014.
Values may be sent and summed in bfloat16 or wider, within the bound.
No kernel may reach another device: no remote copies, remote signals or barrier semaphores. Data moves between devices by JAX's collectives and lax.ppermute only.
A program may use at most 64 MiB of HBM per device.

```python
import math
import jax
import jax.numpy as jnp
import numpy as np
from jax import lax

D = 4096
QH = 32
KVH = 8
HD = 128
SCALES = 8
FINE = 8192
COARSE = 4096


def drawn_keys(key, length, width, salt):
    base = jax.random.truncated_normal(jax.random.fold_in(key, salt), -6.0, 6.0, (length, width), jnp.float32)
    return base


def drawn_queries(key, length, salt_query):
    query = 2.5 * jax.random.truncated_normal(jax.random.fold_in(key, salt_query), -6.0, 6.0, (length, QH * HD), jnp.float32)
    return query


def memory_pair(key, length, salt_keys, salt_values):
    keyset = drawn_keys(key, length, KVH * HD, salt_keys)
    valueset = jax.random.truncated_normal(jax.random.fold_in(key, salt_values), -6.0, 6.0, (length, KVH * HD), jnp.float32)
    return jnp.stack([keyset, valueset]).astype(jnp.bfloat16)


def draw_fine_query(key, part):
    return drawn_queries(key, FINE, 17).astype(jnp.bfloat16)


def draw_fine_memory(key, part):
    return memory_pair(key, FINE, 11, 13)


def draw_coarse_query(key, part):
    return drawn_queries(key, COARSE, 27).astype(jnp.bfloat16)


def draw_coarse_memory(key, part):
    return memory_pair(key, COARSE, 21, 23)


def steps_of(key, extent, split, smallest, largest):
    loudness = 1.0
    for axis_at, blocks in split:
        steps = jax.random.uniform(jax.random.fold_in(jax.random.fold_in(key, 6), axis_at), (blocks,), jnp.float32, smallest / len(split), largest / len(split))
        loudness = loudness * jnp.repeat(jnp.exp(steps), extent[axis_at] // blocks).reshape((-1,) + (1,) * (len(extent) - 1 - axis_at))
    return loudness


def length_profile(count, total, most, lean):
    weights = [(1 << 20) // math.isqrt(rank ** lean) + 1 for rank in range(2, count + 1)]
    surplus, given = total - most - (count - 1), [1] * (count - 1)
    while surplus > 0:
        candidates = [i for i in range(count - 1) if given[i] < most]
        mass, left = sum([weights[i] for i in candidates]), surplus
        for i in candidates:
            extra = min(most - given[i], max(1, left * weights[i] // mass), surplus)
            given[i] = given[i] + extra
            surplus = surplus - extra
    return np.array([most] + given)


def ragged(rng, amount, total, limit, slope):
    if amount == 2:
        one = jax.random.randint(rng, (), max(1, total - limit), min(limit, total - 1) + 1)
        return jnp.stack([one, total - one])
    tallies = jnp.asarray(length_profile(amount, total, limit, slope), jnp.int32)
    couples = (amount - 1) // 2
    source_of, receiver = tallies[1:1 + 2 * couples:2], tallies[2:2 + 2 * couples:2]
    slack = jnp.minimum(source_of - 1, limit - receiver)
    moved = jax.random.randint(jax.random.fold_in(rng, 1), (couples,), 0, 1 << 20) % (slack + 1)
    tallies = tallies.at[1:1 + 2 * couples:2].set(source_of - moved).at[2:2 + 2 * couples:2].set(receiver + moved)
    return tallies[jax.random.permutation(jax.random.fold_in(rng, 2), amount)]


def centred(rng, dims, scale, limit, split=(), dtype=jnp.bfloat16):
    values = jax.random.normal(rng, dims, jnp.float32) * scale
    if len(split) > 0:
        values = steps_of(rng, dims, split, -0.22, 0.18) * values
    return jnp.clip(values, min=-limit, max=limit).astype(dtype)


def setup_inputs(seed: int = 0) -> dict:
    key_of = jax.random.split(jax.random.key(seed), 7)
    fine_query = draw_fine_query(jax.random.fold_in(key_of[6], 71), 0)
    fine_memory = draw_fine_memory(jax.random.fold_in(key_of[6], 71), 0)
    coarse_query = draw_coarse_query(jax.random.fold_in(key_of[6], 71), 0)
    coarse_memory = draw_coarse_memory(jax.random.fold_in(key_of[6], 71), 0)
    coarse_scale = jnp.searchsorted(jnp.cumsum(ragged(key_of[4], SCALES, COARSE, COARSE // 4, 1)), jnp.arange(COARSE), side="right").astype(jnp.int32)
    out_weight = centred(key_of[5], (QH * HD, D), (QH * HD) ** -0.5, 0.09375, ((0, 8),))
    return {"fine_query": fine_query, "fine_memory": fine_memory, "coarse_query": coarse_query, "coarse_memory": coarse_memory, "coarse_scale": coarse_scale, "out_weight": out_weight}


masked_score = -1e30


def attend(queries, key_rows, value_rows, q_level, k_level):
    length = queries.shape[0]
    grouped = queries.astype(jnp.float32).reshape(length, KVH, QH // KVH, HD)
    key_heads = key_rows.astype(jnp.float32).reshape(-1, KVH, HD)
    value_heads = value_rows.astype(jnp.float32).reshape(-1, KVH, HD)
    scores = jnp.einsum('rkgd,skd->kgrs', grouped, key_heads) * (HD ** -0.5)
    allowed = k_level[None, :] <= q_level[:, None]
    scores = jnp.where(allowed[None, None], scores, masked_score)
    highest = jnp.max(scores, axis=-1, keepdims=True)
    shifted = jnp.exp(scores - highest)
    totals = jnp.sum(shifted, axis=-1)
    weights = lax.optimization_barrier(shifted.astype(jnp.bfloat16)).astype(jnp.float32)
    result = jnp.einsum('kgrs,skd->kgrd', weights, value_heads) / totals[..., None]
    return result.transpose(2, 0, 1, 3).reshape(length, QH * HD).astype(jnp.bfloat16)


def run_rows(queries, q_level, key_rows, value_rows, k_level):
    width = queries.shape[1]
    query_blocks = queries.reshape(-1, 64, width)
    level_blocks = q_level.reshape(-1, 64)
    mapped = lax.map(lambda pair: attend(pair[0], key_rows, value_rows, pair[1], k_level), (query_blocks, level_blocks))
    return mapped.reshape(-1, width)


def reference(fine_query, fine_memory, coarse_query, coarse_memory, coarse_scale, out_weight):
    fine_level = jnp.full((FINE,), SCALES, jnp.int32)
    all_keys = jnp.concatenate([fine_memory[0], coarse_memory[0]], axis=0)
    all_values = jnp.concatenate([fine_memory[1], coarse_memory[1]], axis=0)
    all_levels = jnp.concatenate([fine_level, coarse_scale.astype(jnp.int32)], axis=0)
    fine_attention = run_rows(fine_query, fine_level, all_keys, all_values, all_levels)
    coarse_attention = run_rows(coarse_query, coarse_scale.astype(jnp.int32), coarse_memory[0], coarse_memory[1], coarse_scale.astype(jnp.int32))
    fine_mixed = jnp.dot(fine_attention, out_weight, preferred_element_type=jnp.float32).astype(jnp.bfloat16)
    coarse_mixed = jnp.dot(coarse_attention, out_weight, preferred_element_type=jnp.float32).astype(jnp.bfloat16)
    return fine_mixed, coarse_mixed
```

```python
import functools
import math

import jax
import jax.numpy as jnp
from jax import lax
from jax.experimental import pallas as pl
from jax.experimental.pallas import tpu as pltpu
from jax.sharding import Mesh
from jax.sharding import PartitionSpec as P

HD = 128
LEVEL_ROWS = 16
CTX = ("yl", "z", "c")
HEAD = ("yh", "x")
LOW = -1e30
EXPONENT = HD**-0.5 * math.log2(math.e)
NT = (((1,), (1,)), ((), ()))
NN = (((1,), (0,)), ((), ()))


def dot_nt(a, b):
    return lax.dot_general(a, b, NT, preferred_element_type=jnp.float32)


def dot_nn(a, b):
    return lax.dot_general(a, b, NN, preferred_element_type=jnp.float32)


def with_ones(v):
    return jnp.concatenate([v, jnp.ones_like(v)], axis=1)


def rows_of(ref, start, length):
    block = ref[:, start : start + length, :]
    return block.reshape(-1, HD)


def fine_kernel(n_blocks, first, last, tile, q_ref, *refs):
    blocks, refs = refs[:n_blocks], refs[n_blocks:]
    if not first:
        m_in, acc_in, refs = refs[0], refs[1], refs[2:]
    rows, heads = q_ref.shape[0], q_ref.shape[1] // HD
    keys, values = [], []
    for b in blocks:
        length = b.shape[1] // 2 // HD * HD
        keys.append(rows_of(b, 0, length))
        values.append(rows_of(b, length, length))
    k = jnp.concatenate(keys, axis=0)
    v = with_ones(jnp.concatenate(values, axis=0))
    for h in range(heads):
        for r in range(0, rows, tile):
            at = slice(r, r + tile)
            s = dot_nt(q_ref[at, h * HD : (h + 1) * HD], k)
            top = jnp.max(s, axis=1, keepdims=True)
            if first:
                new = jnp.broadcast_to(top, (tile, HD))
            else:
                old = m_in[h, at, :]
                new = jnp.maximum(old, top)
            p = jnp.exp2(s * EXPONENT - new[:, :1] * EXPONENT).astype(jnp.bfloat16)
            acc = dot_nn(p, v)
            if not first:
                acc = acc + acc_in[h, at, :] * jnp.exp2((old - new) * EXPONENT)[:, :1]
            if last:
                refs[0][at, h * HD : (h + 1) * HD] = (acc[:, :HD] / acc[:, HD:]).astype(
                    jnp.bfloat16
                )
            else:
                refs[0][h, at, :] = new
                refs[1][h, at, :] = acc


def whole(shape):
    return pl.BlockSpec(shape, lambda: (0,) * len(shape))


def fine_fold(q, blocks, state, last):
    rows, width = q.shape
    heads = width // HD
    first = state is None
    ins = (q, *blocks, *(() if first else state))
    if last:
        out = jax.ShapeDtypeStruct((rows, width), jnp.bfloat16)
        out_specs = whole(out.shape)
    else:
        out = (
            jax.ShapeDtypeStruct((heads, rows, HD), jnp.float32),
            jax.ShapeDtypeStruct((heads, rows, 2 * HD), jnp.float32),
        )
        out_specs = tuple(whole(o.shape) for o in out)
    n_keys = sum(b.shape[0] * (b.shape[1] // 2 // HD * HD) for b in blocks)
    aliases = {} if first or last else {len(ins) - 2: 0, len(ins) - 1: 1}
    return pl.pallas_call(
        functools.partial(fine_kernel, len(blocks), first, last, math.gcd(rows, 128)),
        out_shape=out,
        in_specs=[whole(a.shape) for a in ins],
        out_specs=out_specs,
        input_output_aliases=aliases,
        compiler_params=pltpu.CompilerParams(vmem_limit_bytes=40 << 20),
        cost_estimate=pl.CostEstimate(
            flops=8 * heads * rows * n_keys * HD,
            bytes_accessed=4 * n_keys * HD + 2 * rows * width,
            transcendentals=heads * rows * n_keys,
        ),
        name="fine_fold",
    )(*ins)


def coarse_kernel(n_blocks, q_ref, level_ref, *refs):
    blocks, o_ref = refs[:n_blocks], refs[n_blocks]
    rows, heads = q_ref.shape[0], q_ref.shape[1] // HD
    length = (blocks[0].shape[1] - LEVEL_ROWS) // 2
    k = jnp.concatenate([rows_of(b, 0, length) for b in blocks], axis=0)
    v = with_ones(jnp.concatenate([rows_of(b, length, length) for b in blocks], axis=0))
    levels = [
        b[i, 2 * length : 2 * length + 1, :] for b in blocks for i in range(b.shape[0])
    ]
    key_level = jnp.concatenate(levels, axis=1).astype(jnp.float32)
    allowed = key_level <= level_ref[:, :1]
    for h in range(heads):
        s = dot_nt(q_ref[:, h * HD : (h + 1) * HD], k)
        s = jnp.where(allowed, s, LOW)
        top = jnp.max(s, axis=1, keepdims=True)
        p = jnp.exp2(s * EXPONENT - top * EXPONENT).astype(jnp.bfloat16)
        acc = dot_nn(p, v)
        o_ref[:, h * HD : (h + 1) * HD] = (acc[:, :HD] / acc[:, HD:]).astype(jnp.bfloat16)


def coarse_attention_of(q, level, blocks):
    rows, width = q.shape
    ins = (q, level, *blocks)
    n_keys = sum(b.shape[0] * HD for b in blocks)
    return pl.pallas_call(
        functools.partial(coarse_kernel, len(blocks)),
        out_shape=jax.ShapeDtypeStruct((rows, width), jnp.bfloat16),
        in_specs=[whole(a.shape) for a in ins],
        out_specs=whole((rows, width)),
        compiler_params=pltpu.CompilerParams(vmem_limit_bytes=40 << 20),
        cost_estimate=pl.CostEstimate(
            flops=8 * rows * width * n_keys,
            bytes_accessed=4 * n_keys * HD + 4 * rows * width,
            transcendentals=rows * width // HD * n_keys,
        ),
        name="coarse_attention",
    )(*ins)


def swapped(x, axis):
    return lax.ppermute(x, axis, [(0, 1), (1, 0)])


def along_z(x):
    n = lax.axis_size("z")
    pairs = []
    for z in range(n):
        pairs.append((2 * z, 2 * ((z + 1) % n)))
        pairs.append((2 * z + 1, 2 * ((z - 1) % n) + 1))
    return lax.ppermute(x, ("z", "c"), pairs)


def ring_gather(piece):
    mine = jnp.stack([piece, swapped(piece, "yl")])
    chip = jnp.concatenate([mine, swapped(mine, "c")], axis=0)
    steps = [(chip,)]
    travelling = chip
    n = lax.axis_size("z")
    for step in range(1, n // 2 + 1):
        if 2 * step == n:
            travelling = travelling[: travelling.shape[0] // 2]
        travelling = along_z(travelling)
        steps.append((travelling, swapped(travelling, "c")))
    return steps


def per_device(fine_query, fine_memory, coarse_query, coarse_memory, coarse_scale, out_weight):
    levels = coarse_scale.astype(jnp.bfloat16)
    level_rows = jnp.broadcast_to(levels[None, :], (LEVEL_ROWS, HD))
    coarse_piece = jnp.concatenate([coarse_memory.reshape(-1, HD), level_rows], axis=0)
    fine_piece = fine_memory.reshape(-1, HD)
    coarse_steps = ring_gather(coarse_piece)
    fine_steps = ring_gather(fine_piece)
    coarse_blocks = [b for step in coarse_steps for b in step]
    query_level = jnp.broadcast_to(coarse_scale.astype(jnp.float32)[:, None], (coarse_scale.shape[0], HD))
    coarse_attention = coarse_attention_of(coarse_query, query_level, coarse_blocks)
    state = fine_fold(fine_query, coarse_blocks, None, False)
    for i, blocks in enumerate(fine_steps):
        state = fine_fold(fine_query, blocks, state, i == len(fine_steps) - 1)
    fine_attention = state
    fine_share = jnp.dot(fine_attention, out_weight, preferred_element_type=jnp.float32)
    coarse_share = jnp.dot(coarse_attention, out_weight, preferred_element_type=jnp.float32)
    n = lax.axis_size(HEAD)

    def exchanged(share):
        share = share.astype(jnp.bfloat16).reshape(n, -1, share.shape[1])
        got = lax.all_to_all(share, HEAD, 0, 0)
        return jnp.sum(got.astype(jnp.float32), axis=0).astype(jnp.bfloat16)

    return exchanged(fine_share), exchanged(coarse_share)


def solution(mesh):
    torus = Mesh(mesh.devices.reshape(2, 8, 2, 2, 4), ("yl", "z", "c", "yh", "x"))
    placed = (
        P(CTX, HEAD),
        P(None, CTX, HEAD),
        P(CTX, HEAD),
        P(None, CTX, HEAD),
        P(CTX),
        P(HEAD, None),
    )
    return jax.shard_map(
        per_device,
        mesh=torus,
        in_specs=placed,
        out_specs=(P(CTX + HEAD, None), P(CTX + HEAD, None)),
        check_vma=False,
    )
```

```python
import functools
import math

import jax
import jax.numpy as jnp
from jax import lax
from jax.experimental import pallas as pl
from jax.experimental.pallas import tpu as pltpu
from jax.sharding import Mesh
from jax.sharding import PartitionSpec as P

HD = 128
PAD = 16
CTX = ("yl", "z", "c")
HEAD = ("yh", "xp", "xl")
LOW = -1e30
EXPONENT = HD**-0.5 * math.log2(math.e)
NT = (((1,), (1,)), ((), ()))
NN = (((1,), (0,)), ((), ()))
GRANT = 24 << 20


def dot_nt(a, b):
    return lax.dot_general(a, b, NT, preferred_element_type=jnp.float32)


def dot_nn(a, b):
    return lax.dot_general(a, b, NN, preferred_element_type=jnp.float32)


def whole(shape):
    return pl.BlockSpec(shape, lambda *_: (0,) * len(shape))


def rows_of(ref, start, length):
    return ref[:, start : start + length, :].reshape(-1, HD)


def in_three(x):
    parts = []
    for _ in range(3):
        part = x.astype(jnp.bfloat16).astype(jnp.float32)
        parts.append(part)
        x = x - part
    return parts


def fold_kernel(n_blocks, fine, coarse, first, last, tile, q_ref, cq_ref, level_ref, *refs):
    blocks, refs = refs[:n_blocks], refs[n_blocks:]
    if not first:
        state, refs = refs[:4], refs[4:]
    heads = q_ref.shape[1] // HD
    at = 2 * fine
    k_fine = [rows_of(b, 0, fine) for b in blocks]
    v_fine = [rows_of(b, fine, fine) for b in blocks]
    k_coarse = [rows_of(b, at, coarse) for b in blocks]
    v_coarse = [rows_of(b, at + coarse, coarse) for b in blocks]
    at = at + 2 * coarse
    key_level = jnp.concatenate(
        [b[i, at : at + 1, :] for b in blocks for i in range(b.shape[0])], axis=1
    ).astype(jnp.float32)
    k = jnp.concatenate(k_fine + k_coarse, axis=0)
    v = jnp.concatenate(v_fine + v_coarse, axis=0)
    v = jnp.concatenate([v, jnp.ones_like(v)], axis=1)
    n_fine = k.shape[0] - key_level.shape[1]

    def attend(queries, keys, values, allowed, h, rows, m_in, acc_in, m_out, acc_out):
        s = dot_nt(queries[rows, h * HD : (h + 1) * HD], keys)
        if allowed is not None:
            s = jnp.where(allowed, s, LOW)
        top = jnp.max(s, axis=1, keepdims=True)
        if first:
            new = jnp.broadcast_to(top, (tile, HD))
        else:
            old = m_in[h, rows, :]
            new = jnp.maximum(old, top)
        p = jnp.exp2(s * EXPONENT - new[:, :1] * EXPONENT).astype(jnp.bfloat16)
        acc = dot_nn(p, values)
        if not first:
            acc = acc + acc_in[h, rows, :] * jnp.exp2((old - new) * EXPONENT)[:, :1]
        if not last:
            m_out[h, rows, :] = new
            acc_out[h, rows, :] = acc
            return None
        total = acc[:, HD : HD + 1]
        return (
            (acc[:, :HD] / acc[:, HD:]).astype(jnp.bfloat16),
            new[:, :1] * EXPONENT + jnp.log(total) * math.log2(math.e),
        )

    lane = lax.broadcasted_iota(jnp.int32, (tile, HD), 1)
    for is_coarse in (False, True):
        queries = cq_ref if is_coarse else q_ref
        pair = 2 if is_coarse else 0
        m_in, acc_in = (None, None) if first else state[pair : pair + 2]
        m_out, acc_out = (None, None) if last else refs[pair : pair + 2]
        for t in range(queries.shape[0] // tile):
            rows = slice(t * tile, (t + 1) * tile)
            if is_coarse:
                allowed = key_level <= level_ref[rows, :1]
                keys, values = k[n_fine:], v[n_fine:]
            else:
                allowed, keys, values = None, k, v
            stats = jnp.zeros((tile, HD), jnp.float32)
            for h in range(heads):
                done = attend(queries, keys, values, allowed, h, rows, m_in, acc_in, m_out, acc_out)
                if last:
                    for i, part in enumerate(in_three(done[1])):
                        stats = jnp.where(lane == 3 * h + i, part, stats)
                    place(refs, is_coarse, t, tile, q_ref.shape[0] // 4, h, done[0])
            if last:
                place(refs, is_coarse, t, tile, q_ref.shape[0] // 4, heads, stats.astype(jnp.bfloat16))


def place(outs, is_coarse, t, tile, n_fine, h, value):
    n = outs[0].shape[0] - n_fine if is_coarse else n_fine
    for i in range(max(1, tile // n)):
        row = t * tile + i * n
        start = row % n + (n_fine if is_coarse else 0)
        length = min(n, tile)
        outs[row // n][start : start + length, h * HD : (h + 1) * HD] = value[
            i * n : i * n + length
        ]


def fold(q, cq, level, blocks, state, last, fine, coarse):
    heads = q.shape[1] // HD
    first = state is None
    ins = (q, cq, level, *blocks, *(() if first else state))
    if last:
        quarter = (q.shape[0] + cq.shape[0]) // 4
        out = (jax.ShapeDtypeStruct((quarter, q.shape[1] + HD), jnp.bfloat16),) * 4
    else:
        out = tuple(
            jax.ShapeDtypeStruct((heads, rows, width), jnp.float32)
            for rows in (q.shape[0], cq.shape[0])
            for width in (HD, 2 * HD)
        )
    n_pieces = sum(b.shape[0] for b in blocks)
    work = heads * n_pieces * (q.shape[0] * (fine + coarse) + cq.shape[0] * coarse)
    aliases = {} if first or last else {len(ins) - 4 + i: i for i in range(4)}
    return pl.pallas_call(
        functools.partial(fold_kernel, len(blocks), fine, coarse, first, last, 128),
        out_shape=out,
        in_specs=[whole(a.shape) for a in ins],
        out_specs=tuple(whole(o.shape) for o in out),
        input_output_aliases=aliases,
        compiler_params=pltpu.CompilerParams(vmem_limit_bytes=GRANT),
        cost_estimate=pl.CostEstimate(
            flops=8 * work * HD, bytes_accessed=4 * q.shape[0] * q.shape[1], transcendentals=work
        ),
        name="fold",
    )(*ins)


def project_kernel(n_fine, n_blocks, core_ref, keep, near, cross, far, w, w_mine, w_other, o_ref, a_ref):
    heads = keep.shape[1] // HD - 1
    rows = keep.shape[0]
    width = heads * HD
    half = width // 2

    @pl.when(pl.program_id(0) == 0)
    def _():
        swap = jnp.broadcast_to(core_ref[0], (1, 1)) == 1
        for g, (one, two) in enumerate(((keep, near), (cross, far))):
            merged = []
            for h in range(heads):
                stat = []
                for ref in (one, two):
                    s = ref[:, width:].astype(jnp.float32)
                    stat.append(s[:, 3 * h : 3 * h + 1] + s[:, 3 * h + 1 : 3 * h + 2] + s[:, 3 * h + 2 : 3 * h + 3])
                top = jnp.maximum(stat[0], stat[1])
                w0, w1 = jnp.exp2(stat[0] - top), jnp.exp2(stat[1] - top)
                cols = slice(h * HD, (h + 1) * HD)
                total = one[:, cols].astype(jnp.float32) * w0 + two[:, cols].astype(jnp.float32) * w1
                merged.append((total / (w0 + w1)).astype(jnp.bfloat16))
            merged = jnp.concatenate(merged, axis=1)
            if g == 1:
                lower, upper = merged[:, :half], merged[:, half:]
                merged = jnp.concatenate(
                    [jnp.where(swap, upper, lower), jnp.where(swap, lower, upper)], axis=1
                )
            n_coarse = rows - n_fine
            f, c = n_fine // n_blocks, n_coarse // n_blocks
            for b in range(n_blocks):
                at = b * (f + c)
                cols = slice(g * width, (g + 1) * width)
                a_ref[at : at + f, cols] = merged[b * f : (b + 1) * f]
                a_ref[at + f : at + f + c, cols] = merged[n_fine + b * c : n_fine + (b + 1) * c]

    o_ref[...] = (
        dot_nn(a_ref[:, :width], w[...])
        + dot_nn(a_ref[:, width : width + half], w_mine[...])
        + dot_nn(a_ref[:, width + half :], w_other[...])
    ).astype(jnp.bfloat16)


def project(core, parts, weights, n_fine, n_blocks):
    rows = parts[0].shape[0]
    columns = weights[0].shape[1]
    tile = math.gcd(columns, 1024)
    depth = sum(w.shape[0] for w in weights)
    return pl.pallas_call(
        functools.partial(project_kernel, n_fine, n_blocks),
        grid=(columns // tile,),
        out_shape=jax.ShapeDtypeStruct((rows, columns), jnp.bfloat16),
        in_specs=[pl.BlockSpec(memory_space=pltpu.SMEM)]
        + [whole(p.shape) for p in parts]
        + [pl.BlockSpec((w.shape[0], tile), lambda j: (0, j)) for w in weights],
        out_specs=pl.BlockSpec((rows, tile), lambda j: (0, j)),
        scratch_shapes=[pltpu.VMEM((rows, depth), jnp.bfloat16)],
        compiler_params=pltpu.CompilerParams(vmem_limit_bytes=GRANT),
        cost_estimate=pl.CostEstimate(
            flops=2 * rows * depth * columns, bytes_accessed=2 * depth * columns, transcendentals=0
        ),
        name="project",
    )(core, *parts, *weights)


def crossed(x, axes):
    n = 2 ** len(axes)
    return lax.ppermute(x, axes, [(i, n - 1 - i) for i in range(n)])


def along_z(x):
    n = lax.axis_size("z")
    pairs = []
    for z in range(n):
        pairs.append((2 * z, 2 * ((z + 1) % n)))
        pairs.append((2 * z + 1, 2 * ((z - 1) % n) + 1))
    return lax.ppermute(x, ("z", "c"), pairs)


def ring_gather(piece):
    travelling = jnp.stack([piece, crossed(piece, ("c",))])
    steps = [(travelling,)]
    n = lax.axis_size("z")
    for step in range(1, n // 2 + 1):
        if 2 * step == n:
            travelling = travelling[: travelling.shape[0] // 2]
        travelling = along_z(travelling)
        steps.append((travelling, crossed(travelling, ("c",))))
    return steps


def near_and_far(rows):
    yh, xp, xl = (lax.axis_size(a) for a in HEAD)
    blocks = rows.reshape(yh * xp, xl, -1, rows.shape[1])
    me = lax.axis_index("xl")
    return [
        lax.dynamic_index_in_dim(blocks, i, 1, keepdims=False).reshape(-1, rows.shape[1])
        for i in (me, 1 - me)
    ]


def per_device(fine_query, fine_memory, coarse_query, coarse_memory, coarse_scale, out_weight):
    fine, coarse = fine_query.shape[0], coarse_query.shape[0]
    width = fine_query.shape[1]
    levels = coarse_scale.astype(jnp.bfloat16)
    level_rows = jnp.broadcast_to(levels[None, :], (PAD, HD))
    piece = jnp.concatenate(
        [fine_memory.reshape(-1, HD), coarse_memory.reshape(-1, HD), level_rows], axis=0
    )
    core = lax.axis_index("c")

    level_columns = jnp.broadcast_to(levels[:, None], (coarse, HD))
    queries = near_and_far(fine_query) + near_and_far(
        jnp.concatenate([coarse_query, level_columns], axis=1)
    )
    fine_mine = jnp.concatenate(queries[:2], axis=0)
    coarse_mine = jnp.concatenate(queries[2:], axis=0)
    fine_theirs = crossed(fine_mine, ("yl",))
    coarse_theirs = crossed(coarse_mine, ("yl",))
    q = jnp.concatenate([fine_mine, fine_theirs], axis=0)
    cq = jnp.concatenate([coarse_mine[:, :width], coarse_theirs[:, :width]], axis=0)
    query_level = jnp.concatenate([coarse_mine[:, width:], coarse_theirs[:, width:]], axis=0).astype(
        jnp.float32
    )

    steps = ring_gather(piece)
    depth = out_weight.shape[0] // 2
    late_core, first = lax.optimization_barrier((core, steps[0][0]))
    steps[0] = (first,)
    weight_mine = crossed(lax.dynamic_slice_in_dim(out_weight, late_core * depth, depth, 0), ("xl",))

    steps = [steps[0] + steps[1]] + steps[2:]
    state = None
    for i, blocks in enumerate(steps):
        state = fold(q, cq, query_level, blocks, state, i == len(steps) - 1, fine, coarse)
    keep, to_xl, to_yl, to_both = state
    weight_mine, keep = lax.optimization_barrier((weight_mine, keep))
    weight_other = crossed(weight_mine, ("c",))
    near = crossed(to_yl, ("yl",))
    far = crossed(to_both, ("yl", "xl"))
    across = crossed(to_xl, ("xl",))
    n = lax.axis_size(HEAD[:2])
    share = project(
        core.reshape(1).astype(jnp.int32),
        (keep, near, across, far),
        (out_weight, weight_mine, weight_other),
        fine // 2,
        n,
    )
    got = lax.all_to_all(share.reshape(n, -1, share.shape[1]), HEAD[:2], 0, 0)
    mixed = jnp.sum(got.astype(jnp.float32), axis=0).astype(jnp.bfloat16)
    split = mixed.shape[0] * fine // (fine + coarse)
    return mixed[:split], mixed[split:]


def solution(mesh):
    torus = Mesh(
        mesh.devices.reshape(2, 8, 2, 2, 2, 2), ("yl", "z", "c", "yh", "xp", "xl")
    )
    placed = (
        P(CTX, HEAD),
        P(None, CTX, HEAD),
        P(CTX, HEAD),
        P(None, CTX, HEAD),
        P(CTX),
        P(HEAD, None),
    )
    return jax.shard_map(
        per_device,
        mesh=torus,
        in_specs=placed,
        out_specs=(P(CTX + HEAD, None), P(CTX + HEAD, None)),
        check_vma=False,
    )
```

```python
import functools
import math

import jax
import jax.numpy as jnp
from jax import lax
from jax.experimental import pallas as pl
from jax.experimental.pallas import tpu as pltpu
from jax.sharding import Mesh
from jax.sharding import PartitionSpec as P

HD = 128
PAD = 16
CTX = ("yl", "z", "c")
HEAD = ("yh", "xp", "xl")
LOW = -1e30
EXPONENT = HD**-0.5 * math.log2(math.e)
NT = (((1,), (1,)), ((), ()))
NN = (((1,), (0,)), ((), ()))
GRANT = 24 << 20
TILE = 256


def dot_nt(a, b):
    return lax.dot_general(a, b, NT, preferred_element_type=jnp.float32)


def dot_nn(a, b):
    return lax.dot_general(a, b, NN, preferred_element_type=jnp.float32)


def whole(shape):
    return pl.BlockSpec(shape, lambda *_: (0,) * len(shape))


def rows_of(ref, start, length):
    return ref[:, start : start + length, :].reshape(-1, HD)


def in_three(x, which):
    result = jnp.zeros_like(x)
    for i in range(3):
        part = x.astype(jnp.bfloat16).astype(jnp.float32)
        result = jnp.where(which == i, part, result)
        x = x - part
    return result.astype(jnp.bfloat16)


def fold_kernel(n_blocks, fine, coarse, first, last, tile, q_ref, cq_ref, level_ref, *refs):
    blocks, refs = refs[:n_blocks], refs[n_blocks:]
    if not first:
        state, refs = refs[:4], refs[4:]
    heads = q_ref.shape[1] // HD
    at = 2 * fine
    k_fine = [rows_of(b, 0, fine) for b in blocks]
    v_fine = [rows_of(b, fine, fine) for b in blocks]
    k_coarse = [rows_of(b, at, coarse) for b in blocks]
    v_coarse = [rows_of(b, at + coarse, coarse) for b in blocks]
    at = at + 2 * coarse
    key_level = jnp.concatenate(
        [b[i, at : at + 1, :] for b in blocks for i in range(b.shape[0])], axis=1
    ).astype(jnp.float32)
    k = jnp.concatenate(k_fine + k_coarse, axis=0)
    v = jnp.concatenate(v_fine + v_coarse, axis=0)
    v = jnp.concatenate([v, jnp.ones_like(v)], axis=1)
    n_fine = k.shape[0] - key_level.shape[1]

    def attend(queries, keys, values, allowed, h, rows, m_in, acc_in, m_out, acc_out):
        s = dot_nt(queries[rows, h * HD : (h + 1) * HD], keys)
        if allowed is not None:
            s = jnp.where(allowed, s, LOW)
        top = jnp.max(s, axis=1, keepdims=True)
        if first:
            new = jnp.broadcast_to(top, (tile, HD))
        else:
            old = m_in[h, rows, :]
            new = jnp.maximum(old, top)
        p = jnp.exp2(s * EXPONENT - new[:, :1] * EXPONENT).astype(jnp.bfloat16)
        acc = dot_nn(p, values)
        if not first:
            acc = acc + acc_in[h, rows, :] * jnp.exp2((old - new) * EXPONENT)[:, :1]
        if not last:
            m_out[h, rows, :] = new
            acc_out[h, rows, :] = acc
            return None
        return (acc[:, :HD] / acc[:, HD:]).astype(jnp.bfloat16), new, acc[:, HD:]

    lane = lax.broadcasted_iota(jnp.int32, (tile, HD), 1)
    for is_coarse in (False, True):
        queries = cq_ref if is_coarse else q_ref
        pair = 2 if is_coarse else 0
        m_in, acc_in = (None, None) if first else state[pair : pair + 2]
        m_out, acc_out = (None, None) if last else refs[pair : pair + 2]
        for t in range(queries.shape[0] // tile):
            rows = slice(t * tile, (t + 1) * tile)
            if is_coarse:
                allowed = key_level <= level_ref[rows, :1]
                keys, values = k[n_fine:], v[n_fine:]
            else:
                allowed, keys, values = None, k, v
            top = jnp.zeros((tile, HD), jnp.float32)
            total = jnp.ones((tile, HD), jnp.float32)
            for h in range(heads):
                done = attend(queries, keys, values, allowed, h, rows, m_in, acc_in, m_out, acc_out)
                if last:
                    place(refs, is_coarse, t, tile, q_ref.shape[0] // 4, h, done[0])
                    top = jnp.where(lane // 3 == h, done[1], top)
                    total = jnp.where(lane // 3 == h, done[2], total)
            if last:
                stats = in_three(top * EXPONENT + jnp.log(total) * math.log2(math.e), lane % 3)
                place(refs, is_coarse, t, tile, q_ref.shape[0] // 4, heads, stats)


def place(outs, is_coarse, t, tile, n_fine, h, value):
    n = outs[0].shape[0] - n_fine if is_coarse else n_fine
    for i in range(max(1, tile // n)):
        row = t * tile + i * n
        start = row % n + (n_fine if is_coarse else 0)
        length = min(n, tile)
        outs[row // n][start : start + length, h * HD : (h + 1) * HD] = value[
            i * n : i * n + length
        ]


def fold(q, cq, level, blocks, state, last, fine, coarse):
    heads = q.shape[1] // HD
    first = state is None
    ins = (q, cq, level, *blocks, *(() if first else state))
    if last:
        quarter = (q.shape[0] + cq.shape[0]) // 4
        out = (jax.ShapeDtypeStruct((quarter, q.shape[1] + HD), jnp.bfloat16),) * 4
    else:
        out = tuple(
            jax.ShapeDtypeStruct((heads, rows, width), jnp.float32)
            for rows in (q.shape[0], cq.shape[0])
            for width in (HD, 2 * HD)
        )
    work = heads * sum(b.shape[0] for b in blocks) * (q.shape[0] * (fine + coarse) + cq.shape[0] * coarse)
    aliases = {} if first or last else {len(ins) - 4 + i: i for i in range(4)}
    return pl.pallas_call(
        functools.partial(fold_kernel, len(blocks), fine, coarse, first, last, TILE),
        out_shape=out,
        in_specs=[whole(a.shape) for a in ins],
        out_specs=tuple(whole(o.shape) for o in out),
        input_output_aliases=aliases,
        compiler_params=pltpu.CompilerParams(vmem_limit_bytes=GRANT),
        cost_estimate=pl.CostEstimate(
            flops=work, bytes_accessed=q.size, transcendentals=0
        ),
        name="fold",
    )(*ins)


def project_kernel(n_fine, n_blocks, core_ref, keep, near, cross, far, w, w_mine, w_other, o_ref, a_ref):
    heads = keep.shape[1] // HD - 1
    rows = keep.shape[0]
    width = heads * HD
    half = width // 2

    @pl.when(pl.program_id(0) == 0)
    def _():
        swap = jnp.broadcast_to(core_ref[0], (1, 1)) == 1
        for g, (one, two) in enumerate(((keep, near), (cross, far))):
            merged = []
            for h in range(heads):
                stat = []
                for ref in (one, two):
                    s = ref[:, width:].astype(jnp.float32)
                    stat.append(s[:, 3 * h : 3 * h + 1] + s[:, 3 * h + 1 : 3 * h + 2] + s[:, 3 * h + 2 : 3 * h + 3])
                top = jnp.maximum(stat[0], stat[1])
                w0, w1 = jnp.exp2(stat[0] - top), jnp.exp2(stat[1] - top)
                cols = slice(h * HD, (h + 1) * HD)
                total = one[:, cols].astype(jnp.float32) * w0 + two[:, cols].astype(jnp.float32) * w1
                merged.append((total / (w0 + w1)).astype(jnp.bfloat16))
            merged = jnp.concatenate(merged, axis=1)
            if g == 1:
                lower, upper = merged[:, :half], merged[:, half:]
                merged = jnp.concatenate(
                    [jnp.where(swap, upper, lower), jnp.where(swap, lower, upper)], axis=1
                )
            n_coarse = rows - n_fine
            f, c = n_fine // n_blocks, n_coarse // n_blocks
            for b in range(n_blocks):
                at = b * (f + c)
                cols = slice(g * width, (g + 1) * width)
                a_ref[at : at + f, cols] = merged[b * f : (b + 1) * f]
                a_ref[at + f : at + f + c, cols] = merged[n_fine + b * c : n_fine + (b + 1) * c]

    o_ref[...] = (
        dot_nn(a_ref[:, :width], w[...])
        + dot_nn(a_ref[:, width : width + half], w_mine[...])
        + dot_nn(a_ref[:, width + half :], w_other[...])
    ).astype(jnp.bfloat16)


def project(core, parts, weights, n_fine, n_blocks):
    rows = parts[0].shape[0]
    columns = weights[0].shape[1]
    tile = math.gcd(columns, 1024)
    depth = sum(w.shape[0] for w in weights)
    return pl.pallas_call(
        functools.partial(project_kernel, n_fine, n_blocks),
        grid=(columns // tile,),
        out_shape=jax.ShapeDtypeStruct((rows, columns), jnp.bfloat16),
        in_specs=[pl.BlockSpec(memory_space=pltpu.SMEM)]
        + [whole(p.shape) for p in parts]
        + [pl.BlockSpec((w.shape[0], tile), lambda j: (0, j)) for w in weights],
        out_specs=pl.BlockSpec((rows, tile), lambda j: (0, j)),
        scratch_shapes=[pltpu.VMEM((rows, depth), jnp.bfloat16)],
        compiler_params=pltpu.CompilerParams(vmem_limit_bytes=GRANT),
        cost_estimate=pl.CostEstimate(
            flops=2 * rows * depth * columns, bytes_accessed=2 * depth * columns, transcendentals=0
        ),
        name="project",
    )(core, *parts, *weights)


def crossed(x, axes):
    n = 2 ** len(axes)
    return lax.ppermute(x, axes, [(i, n - 1 - i) for i in range(n)])


def along_z(x, hops):
    n = lax.axis_size("z")
    pairs = []
    for z in range(n):
        pairs.append((2 * z, 2 * ((z + hops) % n)))
        pairs.append((2 * z + 1, 2 * ((z - hops) % n) + 1))
    return lax.ppermute(x, ("z", "c"), pairs)


def arrange_kernel(n_yh, n_xp, n_xl, xp_ref, fine_mine, fine_theirs, coarse_mine, coarse_theirs, q, cq, level):
    n = n_yh * n_xl
    width = q.shape[1]
    for whose, (fine, coarse) in enumerate(((fine_mine, coarse_mine), (fine_theirs, coarse_theirs))):
        for part in range(2):
            xp = xp_ref[0] if part == 0 else 1 - xp_ref[0]
            for i in range(n):
                block = (i // n_xl * n_xp + xp) * n_xl + i % n_xl
                at = (whose * 2 + part) * n + i
                size = fine.shape[0] // (2 * n)
                start = pl.multiple_of(block * size, size)
                q[at * size : (at + 1) * size, :] = fine[pl.ds(start, size), :]
                size = coarse.shape[0] // (2 * n)
                start = pl.multiple_of(block * size, size)
                rows = coarse[pl.ds(start, size), :]
                cq[at * size : (at + 1) * size, :] = rows[:, :width]
                level[at * size : (at + 1) * size, :] = rows[:, width:].astype(jnp.float32)


def arranged(xp, arrays):
    fine, coarse = arrays[0], arrays[2]
    width = fine.shape[1]
    out = (
        jax.ShapeDtypeStruct((2 * fine.shape[0], width), jnp.bfloat16),
        jax.ShapeDtypeStruct((2 * coarse.shape[0], width), jnp.bfloat16),
        jax.ShapeDtypeStruct((2 * coarse.shape[0], HD), jnp.float32),
    )
    return pl.pallas_call(
        functools.partial(arrange_kernel, *(lax.axis_size(a) for a in HEAD)),
        out_shape=out,
        in_specs=[pl.BlockSpec(memory_space=pltpu.SMEM)] + [whole(a.shape) for a in arrays],
        out_specs=tuple(whole(o.shape) for o in out),
        compiler_params=pltpu.CompilerParams(vmem_limit_bytes=GRANT),
        cost_estimate=pl.CostEstimate(
            flops=0, bytes_accessed=sum(4 * a.size for a in arrays), transcendentals=0
        ),
        name="arrange",
    )(xp, *arrays)


def total_kernel(got, first, second):
    n = first.shape[0]
    total = got[0].astype(jnp.float32)
    for i in range(1, got.shape[0]):
        total = total + got[i].astype(jnp.float32)
    first[...] = total[:n].astype(jnp.bfloat16)
    second[...] = total[n:].astype(jnp.bfloat16)


def totals(got, n):
    parts, rows, columns = got.shape
    tile = math.gcd(columns, 1024)
    return pl.pallas_call(
        functools.partial(total_kernel),
        grid=(columns // tile,),
        out_shape=tuple(
            jax.ShapeDtypeStruct((r, columns), jnp.bfloat16) for r in (n, rows - n)
        ),
        in_specs=[pl.BlockSpec((parts, rows, tile), lambda j: (0, 0, j))],
        out_specs=tuple(pl.BlockSpec((r, tile), lambda j: (0, j)) for r in (n, rows - n)),
        cost_estimate=pl.CostEstimate(flops=got.size, bytes_accessed=3 * got.size, transcendentals=0),
        name="totals",
    )(got)


def per_device(fine_query, fine_memory, coarse_query, coarse_memory, coarse_scale, out_weight):
    fine, coarse = fine_query.shape[0], coarse_query.shape[0]
    width = fine_query.shape[1]
    levels = coarse_scale.astype(jnp.bfloat16)
    level_rows = jnp.broadcast_to(levels[None, :], (PAD, HD))
    piece = jnp.concatenate(
        [fine_memory.reshape(-1, HD), coarse_memory.reshape(-1, HD), level_rows], axis=0
    )
    coarse_mine = jnp.concatenate(
        [coarse_query, jnp.broadcast_to(levels[:, None], (coarse, HD))], axis=1
    )
    fine_theirs = crossed(fine_query, ("yl",))
    coarse_theirs = crossed(coarse_mine, ("yl",))

    chip = jnp.stack([piece, crossed(piece, ("c",))])
    one, two = along_z(chip, 1), along_z(chip, 2)

    core = lax.axis_index("c")
    depth = out_weight.shape[0] // 2
    late_core, chip = lax.optimization_barrier((core, chip))
    weight_mine = crossed(lax.dynamic_slice_in_dim(out_weight, late_core * depth, depth, 0), ("xp",))

    q, cq, query_level = arranged(
        lax.axis_index("xp").reshape(1), (fine_query, fine_theirs, coarse_mine, coarse_theirs)
    )

    def folded(arrivals, state, last):
        blocks = [b for x in arrivals for b in (x, crossed(x, ("c",)))]
        return fold(q, cq, query_level, blocks, state, last, fine, coarse)

    state = fold(q, cq, query_level, [chip], None, False, fine, coarse)
    state, one, two = lax.optimization_barrier((state, one, two))
    three, four = along_z(one, 2), along_z(two[: two.shape[0] // 2], 2)
    state = folded((one, two), state, False)
    state, three, four = lax.optimization_barrier((state, three, four))
    state = folded((three, four), state, True)
    keep, to_xp, to_yl, to_both = state
    weight_mine, keep = lax.optimization_barrier((weight_mine, keep))
    weight_other = crossed(weight_mine, ("c",))
    near = crossed(to_yl, ("yl",))
    far = crossed(to_both, ("yl", "xp"))
    across = crossed(to_xp, ("xp",))
    rest = (HEAD[0], HEAD[2])
    n = lax.axis_size(rest)
    share = project(
        core.reshape(1),
        (keep, near, across, far),
        (out_weight, weight_mine, weight_other),
        fine // 2,
        n,
    )
    got = lax.all_to_all(share.reshape(n, -1, share.shape[1]), rest, 0, 0)
    return totals(got, got.shape[1] * fine // (fine + coarse))


def solution(mesh):
    torus = Mesh(
        mesh.devices.reshape(2, 8, 2, 2, 2, 2), ("yl", "z", "c", "yh", "xp", "xl")
    )
    placed = (
        P(CTX, HEAD),
        P(None, CTX, HEAD),
        P(CTX, HEAD),
        P(None, CTX, HEAD),
        P(CTX),
        P(HEAD, None),
    )
    return jax.shard_map(
        per_device,
        mesh=torus,
        in_specs=placed,
        out_specs=(P(CTX + HEAD, None), P(CTX + HEAD, None)),
        check_vma=False,
    )
```

```python
import functools
import math

import jax
import jax.numpy as jnp
from jax import lax
from jax.experimental import pallas as pl
from jax.experimental.pallas import tpu as pltpu
from jax.sharding import Mesh
from jax.sharding import PartitionSpec as P

HD = 128
PAD = 16
CTX = ("yl", "z", "c")
HEAD = ("yh", "xp", "xl")
LOW = -1e30
EXPONENT = HD**-0.5 * math.log2(math.e)
NT = (((1,), (1,)), ((), ()))
NN = (((1,), (0,)), ((), ()))
GRANT = 24 << 20
TILE = 256


def dot_nt(a, b):
    return lax.dot_general(a, b, NT, preferred_element_type=jnp.float32)


def dot_nn(a, b):
    return lax.dot_general(a, b, NN, preferred_element_type=jnp.float32)


def whole(shape):
    return pl.BlockSpec(shape, lambda *_: (0,) * len(shape))


def rows_of(ref, start, length):
    return ref[:, start : start + length, :].reshape(-1, HD)


def in_three(x, which):
    result = jnp.zeros_like(x)
    for i in range(3):
        part = x.astype(jnp.bfloat16).astype(jnp.float32)
        result = jnp.where(which == i, part, result)
        x = x - part
    return result.astype(jnp.bfloat16)


def fold_kernel(n_blocks, fine, coarse, first, part, q_ref, cq_ref, level_ref, *refs):
    last = part is not None
    blocks, refs = refs[:n_blocks], refs[n_blocks:]
    if not first:
        state, refs = refs[:4], refs[4:]
    heads = q_ref.shape[1] // HD
    at = 2 * fine
    k_fine = [rows_of(b, 0, fine) for b in blocks]
    v_fine = [rows_of(b, fine, fine) for b in blocks]
    k_coarse = [rows_of(b, at, coarse) for b in blocks]
    v_coarse = [rows_of(b, at + coarse, coarse) for b in blocks]
    at = at + 2 * coarse
    key_level = jnp.concatenate(
        [b[i, at : at + 1, :] for b in blocks for i in range(b.shape[0])], axis=1
    ).astype(jnp.float32)
    k = jnp.concatenate(k_fine + k_coarse, axis=0)
    v = jnp.concatenate(v_fine + v_coarse, axis=0)
    v = jnp.concatenate([v, jnp.ones_like(v)], axis=1)
    n_fine = k.shape[0] - key_level.shape[1]

    def attend(queries, keys, values, allowed, h, rows, m_in, acc_in, m_out, acc_out):
        tile = rows.stop - rows.start
        s = dot_nt(queries[rows, h * HD : (h + 1) * HD], keys)
        if allowed is not None:
            s = jnp.where(allowed, s, LOW)
        top = jnp.max(s, axis=1, keepdims=True)
        if first:
            new = jnp.broadcast_to(top, (tile, HD))
        else:
            old = m_in[h, rows, :]
            new = jnp.maximum(old, top)
        p = jnp.exp2(s * EXPONENT - new[:, :1] * EXPONENT).astype(jnp.bfloat16)
        acc = dot_nn(p, values)
        if not first:
            acc = acc + acc_in[h, rows, :] * jnp.exp2((old - new) * EXPONENT)[:, :1]
        if not last:
            m_out[h, rows, :] = new
            acc_out[h, rows, :] = acc
            return None
        return (acc[:, :HD] / acc[:, HD:]).astype(jnp.bfloat16), new, acc[:, HD:]

    for is_coarse in (False, True):
        queries = cq_ref if is_coarse else q_ref
        pair = 2 if is_coarse else 0
        m_in, acc_in = (None, None) if first else state[pair : pair + 2]
        m_out, acc_out = (None, None) if last else refs[pair : pair + 2]
        half = queries.shape[0] // 2
        tile = min(TILE, half)
        lane = lax.broadcasted_iota(jnp.int32, (tile, HD), 1)
        begin, end = (part * half, (part + 1) * half) if last else (0, 2 * half)
        for start in range(begin, end, tile):
            rows = slice(start, start + tile)
            if is_coarse:
                allowed = key_level <= level_ref[rows, :1]
                keys, values = k[n_fine:], v[n_fine:]
            else:
                allowed, keys, values = None, k, v
            top = jnp.zeros((tile, HD), jnp.float32)
            total = jnp.ones((tile, HD), jnp.float32)
            for h in range(heads):
                done = attend(queries, keys, values, allowed, h, rows, m_in, acc_in, m_out, acc_out)
                if last:
                    place(refs, is_coarse, start - begin, q_ref.shape[0] // 4, h, done[0])
                    top = jnp.where(lane // 3 == h, done[1], top)
                    total = jnp.where(lane // 3 == h, done[2], total)
            if last:
                stats = in_three(top * EXPONENT + jnp.log(total) * math.log2(math.e), lane % 3)
                place(refs, is_coarse, start - begin, q_ref.shape[0] // 4, heads, stats)


def place(outs, is_coarse, begin, n_fine, h, value):
    n = outs[0].shape[0] - n_fine if is_coarse else n_fine
    length = min(n, value.shape[0])
    for i in range(value.shape[0] // length):
        row = begin + i * length
        start = row % n + (n_fine if is_coarse else 0)
        outs[row // n][start : start + length, h * HD : (h + 1) * HD] = value[
            i * length : (i + 1) * length
        ]


def fold(q, cq, level, blocks, state, part, fine, coarse):
    heads = q.shape[1] // HD
    first = state is None
    ins = (q, cq, level, *blocks, *(() if first else state))
    last = part is not None
    if last:
        quarter = (q.shape[0] + cq.shape[0]) // 4
        out = (jax.ShapeDtypeStruct((quarter, q.shape[1] + HD), jnp.bfloat16),) * 2
    else:
        out = tuple(
            jax.ShapeDtypeStruct((heads, rows, width), jnp.float32)
            for rows in (q.shape[0], cq.shape[0])
            for width in (HD, 2 * HD)
        )
    work = heads * sum(b.shape[0] for b in blocks) * (q.shape[0] * (fine + coarse) + cq.shape[0] * coarse)
    aliases = {} if first or last else {len(ins) - 4 + i: i for i in range(4)}
    return pl.pallas_call(
        functools.partial(fold_kernel, len(blocks), fine, coarse, first, part),
        out_shape=out,
        in_specs=[whole(a.shape) for a in ins],
        out_specs=tuple(whole(o.shape) for o in out),
        input_output_aliases=aliases,
        compiler_params=pltpu.CompilerParams(vmem_limit_bytes=GRANT),
        cost_estimate=pl.CostEstimate(
            flops=8 * work * HD, bytes_accessed=q.size, transcendentals=0
        ),
        name="fold",
    )(*ins)


def project_kernel(n_fine, n_blocks, place_ref, keep, near, cross, far, w, w_mine, w_other, *refs):
    outs, a_ref = refs[:-1], refs[-1]
    heads = keep.shape[1] // HD - 1
    rows = keep.shape[0]
    width = heads * HD
    half = width // 2

    @pl.when(pl.program_id(0) == 0)
    def _():
        swap = jnp.broadcast_to(place_ref[0], (1, 1)) == 1
        for g, (one, two) in enumerate(((keep, near), (cross, far))):
            merged = []
            for h in range(heads):
                stat = []
                for ref in (one, two):
                    s = ref[:, width:].astype(jnp.float32)
                    stat.append(s[:, 3 * h : 3 * h + 1] + s[:, 3 * h + 1 : 3 * h + 2] + s[:, 3 * h + 2 : 3 * h + 3])
                top = jnp.maximum(stat[0], stat[1])
                w0, w1 = jnp.exp2(stat[0] - top), jnp.exp2(stat[1] - top)
                cols = slice(h * HD, (h + 1) * HD)
                total = one[:, cols].astype(jnp.float32) * w0 + two[:, cols].astype(jnp.float32) * w1
                merged.append((total / (w0 + w1)).astype(jnp.bfloat16))
            merged = jnp.concatenate(merged, axis=1)
            if g == 1:
                lower, upper = merged[:, :half], merged[:, half:]
                merged = jnp.concatenate(
                    [jnp.where(swap, upper, lower), jnp.where(swap, lower, upper)], axis=1
                )
            n_coarse = rows - n_fine
            f, c = n_fine // n_blocks, n_coarse // n_blocks
            for b in range(n_blocks):
                at = jnp.bitwise_xor(place_ref[1], b) * (f + c)
                cols = slice(g * width, (g + 1) * width)
                a_ref[pl.ds(pl.multiple_of(at, c), f), cols] = merged[b * f : (b + 1) * f]
                a_ref[pl.ds(pl.multiple_of(at + f, c), c), cols] = merged[
                    n_fine + b * c : n_fine + (b + 1) * c
                ]

    share = (
        dot_nn(a_ref[:, :width], w[...])
        + dot_nn(a_ref[:, width : width + half], w_mine[...])
        + dot_nn(a_ref[:, width + half :], w_other[...])
    ).astype(jnp.bfloat16)
    size = rows // n_blocks
    for i, out in enumerate(outs):
        out[...] = share[i * size : (i + 1) * size]


def project(places, parts, weights, n_fine, n_blocks):
    rows = parts[0].shape[0]
    columns = weights[0].shape[1]
    tile = math.gcd(columns, 1024)
    depth = sum(w.shape[0] for w in weights)
    return pl.pallas_call(
        functools.partial(project_kernel, n_fine, n_blocks),
        grid=(columns // tile,),
        out_shape=(jax.ShapeDtypeStruct((rows // n_blocks, columns), jnp.bfloat16),) * n_blocks,
        in_specs=[pl.BlockSpec(memory_space=pltpu.SMEM)]
        + [whole(p.shape) for p in parts]
        + [pl.BlockSpec((w.shape[0], tile), lambda j: (0, j)) for w in weights],
        out_specs=(pl.BlockSpec((rows // n_blocks, tile), lambda j: (0, j)),) * n_blocks,
        scratch_shapes=[pltpu.VMEM((rows, depth), jnp.bfloat16)],
        compiler_params=pltpu.CompilerParams(vmem_limit_bytes=GRANT),
        cost_estimate=pl.CostEstimate(
            flops=2 * rows * depth * columns, bytes_accessed=2 * depth * columns, transcendentals=0
        ),
        name="project",
    )(places, *parts, *weights)


def crossed(x, axes):
    n = 2 ** len(axes)
    return lax.ppermute(x, axes, [(i, n - 1 - i) for i in range(n)])


def along_z(x, hops):
    n = lax.axis_size("z")
    pairs = []
    for z in range(n):
        pairs.append((2 * z, 2 * ((z + hops) % n)))
        pairs.append((2 * z + 1, 2 * ((z - hops) % n) + 1))
    return lax.ppermute(x, ("z", "c"), pairs)


def arrange_kernel(n_yh, n_xp, n_xl, xp_ref, fine_mine, fine_theirs, coarse_mine, coarse_theirs, q, cq, level):
    n = n_yh * n_xl
    width = q.shape[1]
    for whose, (fine, coarse) in enumerate(((fine_mine, coarse_mine), (fine_theirs, coarse_theirs))):
        for part in range(2):
            xp = xp_ref[0] if part == 0 else 1 - xp_ref[0]
            for i in range(n):
                block = (i // n_xl * n_xp + xp) * n_xl + i % n_xl
                at = (whose * 2 + part) * n + i
                size = fine.shape[0] // (2 * n)
                start = pl.multiple_of(block * size, size)
                q[at * size : (at + 1) * size, :] = fine[pl.ds(start, size), :]
                size = coarse.shape[0] // (2 * n)
                start = pl.multiple_of(block * size, size)
                rows = coarse[pl.ds(start, size), :]
                cq[at * size : (at + 1) * size, :] = rows[:, :width]
                level[at * size : (at + 1) * size, :] = rows[:, width:].astype(jnp.float32)


def arranged(xp, arrays):
    fine, coarse = arrays[0], arrays[2]
    width = fine.shape[1]
    out = (
        jax.ShapeDtypeStruct((2 * fine.shape[0], width), jnp.bfloat16),
        jax.ShapeDtypeStruct((2 * coarse.shape[0], width), jnp.bfloat16),
        jax.ShapeDtypeStruct((2 * coarse.shape[0], HD), jnp.float32),
    )
    return pl.pallas_call(
        functools.partial(arrange_kernel, *(lax.axis_size(a) for a in HEAD)),
        out_shape=out,
        in_specs=[pl.BlockSpec(memory_space=pltpu.SMEM)] + [whole(a.shape) for a in arrays],
        out_specs=tuple(whole(o.shape) for o in out),
        compiler_params=pltpu.CompilerParams(vmem_limit_bytes=GRANT),
        cost_estimate=pl.CostEstimate(
            flops=0, bytes_accessed=sum(4 * a.size for a in arrays), transcendentals=0
        ),
        name="arrange",
    )(xp, *arrays)


def per_device(fine_query, fine_memory, coarse_query, coarse_memory, coarse_scale, out_weight):
    fine, coarse = fine_query.shape[0], coarse_query.shape[0]
    width = fine_query.shape[1]
    levels = coarse_scale.astype(jnp.bfloat16)
    level_rows = jnp.broadcast_to(levels[None, :], (PAD, HD))
    piece = jnp.concatenate(
        [fine_memory.reshape(-1, HD), coarse_memory.reshape(-1, HD), level_rows], axis=0
    )
    coarse_mine = jnp.concatenate(
        [coarse_query, jnp.broadcast_to(levels[:, None], (coarse, HD))], axis=1
    )
    fine_theirs = crossed(fine_query, ("yl",))
    coarse_theirs = crossed(coarse_mine, ("yl",))

    chip = jnp.stack([piece, crossed(piece, ("c",))])
    one, two = along_z(chip, 1), along_z(chip, 2)

    core = lax.axis_index("c")
    depth = out_weight.shape[0] // 2
    weight_mine = crossed(lax.dynamic_slice_in_dim(out_weight, core * depth, depth, 0), ("xp",))

    q, cq, query_level = arranged(
        lax.axis_index("xp").reshape(1), (fine_query, fine_theirs, coarse_mine, coarse_theirs)
    )

    def folded(blocks, state, part):
        return fold(q, cq, query_level, blocks, state, part, fine, coarse)

    def with_twins(arrivals):
        return [b for x in arrivals for b in (x, crossed(x, ("c",)))]

    state = folded([chip], None, None)
    state, one, two = lax.optimization_barrier((state, one, two))
    three, four = along_z(one, 2), along_z(two[: two.shape[0] // 2], 2)
    state = folded(with_twins((one, two)), state, None)
    state, three, four = lax.optimization_barrier((state, three, four))
    blocks = with_twins((three, four))
    to_yl, to_both = folded(blocks, state, 1)
    near, far = crossed(to_yl, ("yl",)), crossed(to_both, ("yl", "xp"))
    keep, to_xp = folded(blocks, state, 0)
    across = crossed(to_xp, ("xp",))
    weight_mine, keep = lax.optimization_barrier((weight_mine, keep))
    weight_other = crossed(weight_mine, ("c",))
    shares = project(
        jnp.stack([core, lax.axis_index((HEAD[0], HEAD[2]))]),
        (keep, near, across, far),
        (out_weight, weight_mine, weight_other),
        fine // 2,
        4,
    )
    got = [shares[0]]
    for share, axes in zip(shares[1:], ((HEAD[2],), (HEAD[0],), (HEAD[0], HEAD[2]))):
        got.append(crossed(share, axes))
    split = got[0].shape[0] * fine // (fine + coarse)

    def total(rows):
        return sum(g[rows].astype(jnp.float32) for g in got).astype(jnp.bfloat16)

    return total(slice(0, split)), total(slice(split, None))


def solution(mesh):
    torus = Mesh(
        mesh.devices.reshape(2, 8, 2, 2, 2, 2), ("yl", "z", "c", "yh", "xp", "xl")
    )
    placed = (
        P(CTX, HEAD),
        P(None, CTX, HEAD),
        P(CTX, HEAD),
        P(None, CTX, HEAD),
        P(CTX),
        P(HEAD, None),
    )
    return jax.shard_map(
        per_device,
        mesh=torus,
        in_specs=placed,
        out_specs=(P(CTX + HEAD, None), P(CTX + HEAD, None)),
        check_vma=False,
    )
```

```python
import functools
import math

import jax
import jax.numpy as jnp
from jax import lax
from jax.experimental import pallas as pl
from jax.experimental.pallas import tpu as pltpu
from jax.sharding import Mesh
from jax.sharding import PartitionSpec as P

HD = 128
PAD = 16
CTX = ("yl", "z", "c")
HEAD = ("yh", "xp", "xl")
LOW = -1e30
EXPONENT = HD**-0.5 * math.log2(math.e)
NT = (((1,), (1,)), ((), ()))
NN = (((1,), (0,)), ((), ()))
GRANT = 24 << 20
TILE = 256


def dot_nt(a, b):
    return lax.dot_general(a, b, NT, preferred_element_type=jnp.float32)


def dot_nn(a, b):
    return lax.dot_general(a, b, NN, preferred_element_type=jnp.float32)


def whole(shape):
    return pl.BlockSpec(shape, lambda *_: (0,) * len(shape))


def rows_of(ref, start, length):
    return ref[:, start : start + length, :].reshape(-1, HD)


def in_three(x, which):
    result = jnp.zeros_like(x)
    for i in range(3):
        part = x.astype(jnp.bfloat16).astype(jnp.float32)
        result = jnp.where(which == i, part, result)
        x = x - part
    return result.astype(jnp.bfloat16)


def fold_kernel(n_blocks, fine, coarse, first, part, q_ref, cq_ref, level_ref, *refs):
    last = part is not None
    blocks, refs = refs[:n_blocks], refs[n_blocks:]
    if not first:
        state, refs = refs[:4], refs[4:]
    heads = q_ref.shape[1] // HD
    at = 2 * fine
    k_fine = [rows_of(b, 0, fine) for b in blocks]
    v_fine = [rows_of(b, fine, fine) for b in blocks]
    k_coarse = [rows_of(b, at, coarse) for b in blocks]
    v_coarse = [rows_of(b, at + coarse, coarse) for b in blocks]
    at = at + 2 * coarse
    key_level = jnp.concatenate(
        [b[i, at : at + 1, :] for b in blocks for i in range(b.shape[0])], axis=1
    ).astype(jnp.float32)
    k = jnp.concatenate(k_fine + k_coarse, axis=0)
    v = jnp.concatenate(v_fine + v_coarse, axis=0)
    v = jnp.concatenate([v, jnp.ones_like(v)], axis=1)
    n_fine = k.shape[0] - key_level.shape[1]

    def attend(queries, keys, values, allowed, h, rows, m_in, acc_in, m_out, acc_out):
        tile = rows.stop - rows.start
        s = dot_nt(queries[rows, h * HD : (h + 1) * HD], keys)
        if allowed is not None:
            s = jnp.where(allowed, s, LOW)
        top = jnp.max(s, axis=1, keepdims=True)
        if first:
            new = jnp.broadcast_to(top, (tile, HD))
        else:
            old = m_in[h, rows, :]
            new = jnp.maximum(old, top)
        p = jnp.exp2(s * EXPONENT - new[:, :1] * EXPONENT).astype(jnp.bfloat16)
        acc = dot_nn(p, values)
        if not first:
            acc = acc + acc_in[h, rows, :] * jnp.exp2((old - new) * EXPONENT)[:, :1]
        if not last:
            m_out[h, rows, :] = new
            acc_out[h, rows, :] = acc
            return None
        return (acc[:, :HD] / acc[:, HD:]).astype(jnp.bfloat16), new, acc[:, HD:]

    for is_coarse in (False, True):
        queries = cq_ref if is_coarse else q_ref
        pair = 2 if is_coarse else 0
        m_in, acc_in = (None, None) if first else state[pair : pair + 2]
        m_out, acc_out = (None, None) if last else refs[pair : pair + 2]
        half = queries.shape[0] // 2
        tile = min(TILE, half)
        lane = lax.broadcasted_iota(jnp.int32, (tile, HD), 1)
        begin, end = (part * half, (part + 1) * half) if last else (0, 2 * half)
        for start in range(begin, end, tile):
            rows = slice(start, start + tile)
            if is_coarse:
                allowed = key_level <= level_ref[rows, :1]
                keys, values = k[n_fine:], v[n_fine:]
            else:
                allowed, keys, values = None, k, v
            top = jnp.zeros((tile, HD), jnp.float32)
            total = jnp.ones((tile, HD), jnp.float32)
            for h in range(heads):
                done = attend(queries, keys, values, allowed, h, rows, m_in, acc_in, m_out, acc_out)
                if last:
                    place(refs, is_coarse, start - begin, q_ref.shape[0] // 4, h, done[0])
                    top = jnp.where(lane // 3 == h, done[1], top)
                    total = jnp.where(lane // 3 == h, done[2], total)
            if last:
                stats = in_three(top * EXPONENT + jnp.log(total) * math.log2(math.e), lane % 3)
                place(refs, is_coarse, start - begin, q_ref.shape[0] // 4, heads, stats)


def place(outs, is_coarse, begin, n_fine, h, value):
    n = outs[0].shape[0] - n_fine if is_coarse else n_fine
    length = min(n, value.shape[0])
    for i in range(value.shape[0] // length):
        row = begin + i * length
        start = row % n + (n_fine if is_coarse else 0)
        outs[row // n][start : start + length, h * HD : (h + 1) * HD] = value[
            i * length : (i + 1) * length
        ]


def fold(q, cq, level, blocks, state, part, fine, coarse):
    heads = q.shape[1] // HD
    first = state is None
    ins = (q, cq, level, *blocks, *(() if first else state))
    last = part is not None
    if last:
        quarter = (q.shape[0] + cq.shape[0]) // 4
        out = (jax.ShapeDtypeStruct((quarter, q.shape[1] + HD), jnp.bfloat16),) * 2
    else:
        out = tuple(
            jax.ShapeDtypeStruct((heads, rows, width), jnp.float32)
            for rows in (q.shape[0], cq.shape[0])
            for width in (HD, 2 * HD)
        )
    work = heads * sum(b.shape[0] for b in blocks) * (q.shape[0] * (fine + coarse) + cq.shape[0] * coarse)
    aliases = {} if first or last else {len(ins) - 4 + i: i for i in range(4)}
    return pl.pallas_call(
        functools.partial(fold_kernel, len(blocks), fine, coarse, first, part),
        out_shape=out,
        in_specs=[whole(a.shape) for a in ins],
        out_specs=tuple(whole(o.shape) for o in out),
        input_output_aliases=aliases,
        compiler_params=pltpu.CompilerParams(vmem_limit_bytes=GRANT),
        cost_estimate=pl.CostEstimate(
            flops=(1 if last else 8) * work * HD, bytes_accessed=q.size, transcendentals=0
        ),
        name="fold",
    )(*ins)


def project_kernel(n_fine, n_blocks, place_ref, keep, near, cross, far, w, w_mine, w_other, *refs):
    outs, a_ref = refs[:-1], refs[-1]
    heads = keep.shape[1] // HD - 1
    rows = keep.shape[0]
    width = heads * HD
    half = width // 2

    @pl.when(pl.program_id(0) == 0)
    def _():
        swap = jnp.broadcast_to(place_ref[0], (1, 1)) == 1
        for g, (one, two) in enumerate(((keep, near), (cross, far))):
            merged = []
            for h in range(heads):
                stat = []
                for ref in (one, two):
                    s = ref[:, width:].astype(jnp.float32)
                    stat.append(s[:, 3 * h : 3 * h + 1] + s[:, 3 * h + 1 : 3 * h + 2] + s[:, 3 * h + 2 : 3 * h + 3])
                top = jnp.maximum(stat[0], stat[1])
                w0, w1 = jnp.exp2(stat[0] - top), jnp.exp2(stat[1] - top)
                cols = slice(h * HD, (h + 1) * HD)
                total = one[:, cols].astype(jnp.float32) * w0 + two[:, cols].astype(jnp.float32) * w1
                merged.append((total / (w0 + w1)).astype(jnp.bfloat16))
            merged = jnp.concatenate(merged, axis=1)
            if g == 1:
                lower, upper = merged[:, :half], merged[:, half:]
                merged = jnp.concatenate(
                    [jnp.where(swap, upper, lower), jnp.where(swap, lower, upper)], axis=1
                )
            n_coarse = rows - n_fine
            f, c = n_fine // n_blocks, n_coarse // n_blocks
            for b in range(n_blocks):
                at = jnp.bitwise_xor(place_ref[1], b) * (f + c)
                cols = slice(g * width, (g + 1) * width)
                a_ref[pl.ds(pl.multiple_of(at, c), f), cols] = merged[b * f : (b + 1) * f]
                a_ref[pl.ds(pl.multiple_of(at + f, c), c), cols] = merged[
                    n_fine + b * c : n_fine + (b + 1) * c
                ]

    share = (
        dot_nn(a_ref[:, :width], w[...])
        + dot_nn(a_ref[:, width : width + half], w_mine[...])
        + dot_nn(a_ref[:, width + half :], w_other[...])
    ).astype(jnp.bfloat16)
    size = rows // n_blocks
    for i, out in enumerate(outs):
        out[...] = share[i * size : (i + 1) * size]


def project(places, parts, weights, n_fine, n_blocks):
    rows = parts[0].shape[0]
    columns = weights[0].shape[1]
    tile = math.gcd(columns, 1024)
    depth = sum(w.shape[0] for w in weights)
    return pl.pallas_call(
        functools.partial(project_kernel, n_fine, n_blocks),
        grid=(columns // tile,),
        out_shape=(jax.ShapeDtypeStruct((rows // n_blocks, columns), jnp.bfloat16),) * n_blocks,
        in_specs=[pl.BlockSpec(memory_space=pltpu.SMEM)]
        + [whole(p.shape) for p in parts]
        + [pl.BlockSpec((w.shape[0], tile), lambda j: (0, j)) for w in weights],
        out_specs=(pl.BlockSpec((rows // n_blocks, tile), lambda j: (0, j)),) * n_blocks,
        scratch_shapes=[pltpu.VMEM((rows, depth), jnp.bfloat16)],
        compiler_params=pltpu.CompilerParams(vmem_limit_bytes=GRANT),
        cost_estimate=pl.CostEstimate(
            flops=2 * rows * depth * columns, bytes_accessed=2 * depth * columns, transcendentals=0
        ),
        name="project",
    )(places, *parts, *weights)


def crossed(x, axes):
    n = 2 ** len(axes)
    return lax.ppermute(x, axes, [(i, n - 1 - i) for i in range(n)])


def along_z(x, hops):
    n = lax.axis_size("z")
    pairs = []
    for z in range(n):
        pairs.append((2 * z, 2 * ((z + hops) % n)))
        pairs.append((2 * z + 1, 2 * ((z - hops) % n) + 1))
    return lax.ppermute(x, ("z", "c"), pairs)


def arrange_kernel(n_yh, n_xp, n_xl, xp_ref, fine_mine, fine_theirs, coarse_mine, coarse_theirs, q, cq, level):
    n = n_yh * n_xl
    width = q.shape[1]
    for whose, (fine, coarse) in enumerate(((fine_mine, coarse_mine), (fine_theirs, coarse_theirs))):
        for part in range(2):
            xp = xp_ref[0] if part == 0 else 1 - xp_ref[0]
            for i in range(n):
                block = (i // n_xl * n_xp + xp) * n_xl + i % n_xl
                at = (whose * 2 + part) * n + i
                size = fine.shape[0] // (2 * n)
                start = pl.multiple_of(block * size, size)
                q[at * size : (at + 1) * size, :] = fine[pl.ds(start, size), :]
                size = coarse.shape[0] // (2 * n)
                start = pl.multiple_of(block * size, size)
                rows = coarse[pl.ds(start, size), :]
                cq[at * size : (at + 1) * size, :] = rows[:, :width]
                level[at * size : (at + 1) * size, :] = rows[:, width:].astype(jnp.float32)


def arranged(xp, arrays):
    fine, coarse = arrays[0], arrays[2]
    width = fine.shape[1]
    out = (
        jax.ShapeDtypeStruct((2 * fine.shape[0], width), jnp.bfloat16),
        jax.ShapeDtypeStruct((2 * coarse.shape[0], width), jnp.bfloat16),
        jax.ShapeDtypeStruct((2 * coarse.shape[0], HD), jnp.float32),
    )
    return pl.pallas_call(
        functools.partial(arrange_kernel, *(lax.axis_size(a) for a in HEAD)),
        out_shape=out,
        in_specs=[pl.BlockSpec(memory_space=pltpu.SMEM)] + [whole(a.shape) for a in arrays],
        out_specs=tuple(whole(o.shape) for o in out),
        compiler_params=pltpu.CompilerParams(vmem_limit_bytes=GRANT),
        cost_estimate=pl.CostEstimate(
            flops=0, bytes_accessed=sum(4 * a.size for a in arrays), transcendentals=0
        ),
        name="arrange",
    )(xp, *arrays)


def after_kernel(*refs):
    pltpu.touch(refs[-1])


def after(x, before):
    return pl.pallas_call(
        after_kernel,
        out_shape=jax.ShapeDtypeStruct(x.shape, x.dtype),
        in_specs=[pl.BlockSpec(memory_space=pl.ANY)] * (1 + len(before)),
        out_specs=pl.BlockSpec(memory_space=pl.ANY),
        input_output_aliases={0: 0},
        compiler_params=pltpu.CompilerParams(vmem_limit_bytes=1 << 20),
        name="after",
    )(x, *before)


def per_device(fine_query, fine_memory, coarse_query, coarse_memory, coarse_scale, out_weight):
    fine, coarse = fine_query.shape[0], coarse_query.shape[0]
    width = fine_query.shape[1]
    levels = coarse_scale.astype(jnp.bfloat16)
    level_rows = jnp.broadcast_to(levels[None, :], (PAD, HD))
    piece = jnp.concatenate(
        [fine_memory.reshape(-1, HD), coarse_memory.reshape(-1, HD), level_rows], axis=0
    )
    coarse_mine = jnp.concatenate(
        [coarse_query, jnp.broadcast_to(levels[:, None], (coarse, HD))], axis=1
    )
    fine_theirs = crossed(fine_query, ("yl",))
    coarse_theirs = crossed(coarse_mine, ("yl",))

    chip = jnp.stack([piece, crossed(piece, ("c",))])
    one, two = along_z(chip, 1), along_z(chip, 2)

    core = lax.axis_index("c")
    depth = out_weight.shape[0] // 2
    weight_mine = crossed(lax.dynamic_slice_in_dim(out_weight, core * depth, depth, 0), ("xp",))

    q, cq, query_level = arranged(
        lax.axis_index("xp").reshape(1), (fine_query, fine_theirs, coarse_mine, coarse_theirs)
    )

    def folded(blocks, state, part):
        return fold(q, cq, query_level, blocks, state, part, fine, coarse)

    def with_twins(arrivals):
        return [b for x in arrivals for b in (x, crossed(x, ("c",)))]

    state = folded([chip], None, None)
    state, one, two = lax.optimization_barrier((state, one, two))
    three, four = along_z(one, 2), along_z(two[: two.shape[0] // 2], 2)
    state = folded(with_twins((one, two)), state, None)
    state, three, four = lax.optimization_barrier((state, three, four))
    blocks = with_twins((three, four))
    to_yl, to_both = folded(blocks, state, 1)
    near, far = crossed(to_yl, ("yl",)), crossed(to_both, ("yl", "xp"))
    keep, to_xp = folded(blocks, state, 0)
    across = crossed(to_xp, ("xp",))
    weight_mine = after(weight_mine, (near, far, across))
    weight_other = crossed(weight_mine, ("c",))
    shares = project(
        jnp.stack([core, lax.axis_index((HEAD[0], HEAD[2]))]),
        (keep, near, across, far),
        (out_weight, weight_mine, weight_other),
        fine // 2,
        4,
    )
    got = [shares[0]]
    for share, axes in zip(shares[1:], ((HEAD[2],), (HEAD[0],), (HEAD[0], HEAD[2]))):
        got.append(crossed(share, axes))
    split = got[0].shape[0] * fine // (fine + coarse)

    def total(rows):
        return sum(g[rows].astype(jnp.float32) for g in got).astype(jnp.bfloat16)

    return total(slice(0, split)), total(slice(split, None))


def solution(mesh):
    torus = Mesh(
        mesh.devices.reshape(2, 8, 2, 2, 2, 2), ("yl", "z", "c", "yh", "xp", "xl")
    )
    placed = (
        P(CTX, HEAD),
        P(None, CTX, HEAD),
        P(CTX, HEAD),
        P(None, CTX, HEAD),
        P(CTX),
        P(HEAD, None),
    )
    return jax.shard_map(
        per_device,
        mesh=torus,
        in_specs=placed,
        out_specs=(P(CTX + HEAD, None), P(CTX + HEAD, None)),
        check_vma=False,
    )
```

```python
import functools
import math

import jax
import jax.numpy as jnp
from jax import lax
from jax.experimental import pallas as pl
from jax.experimental.pallas import tpu as pltpu
from jax.sharding import Mesh
from jax.sharding import PartitionSpec as P

HD = 128
PAD = 16
CTX = ("yl", "z", "c")
HEAD = ("yh", "xp", "xl")
LOW = -1e30
EXPONENT = HD**-0.5 * math.log2(math.e)
NT = (((1,), (1,)), ((), ()))
NN = (((1,), (0,)), ((), ()))
GRANT = 24 << 20
TILE = 256


def dot_nt(a, b):
    return lax.dot_general(a, b, NT, preferred_element_type=jnp.float32)


def dot_nn(a, b):
    return lax.dot_general(a, b, NN, preferred_element_type=jnp.float32)


def whole(shape):
    return pl.BlockSpec(shape, lambda *_: (0,) * len(shape))


def rows_of(ref, start, length):
    return ref[:, start : start + length, :].reshape(-1, HD)


def in_three(x, which):
    result = jnp.zeros_like(x)
    for i in range(3):
        part = x.astype(jnp.bfloat16).astype(jnp.float32)
        result = jnp.where(which == i, part, result)
        x = x - part
    return result.astype(jnp.bfloat16)


def fold_kernel(n_blocks, fine, coarse, first, part, q_ref, cq_ref, level_ref, *refs):
    last = part is not None
    blocks, refs = refs[:n_blocks], refs[n_blocks:]
    if not first:
        state, refs = refs[:4], refs[4:]
    heads = q_ref.shape[1] // HD
    at = 2 * fine
    k_fine = [rows_of(b, 0, fine) for b in blocks]
    v_fine = [rows_of(b, fine, fine) for b in blocks]
    k_coarse = [rows_of(b, at, coarse) for b in blocks]
    v_coarse = [rows_of(b, at + coarse, coarse) for b in blocks]
    at = at + 2 * coarse
    key_level = jnp.concatenate(
        [b[i, at : at + 1, :] for b in blocks for i in range(b.shape[0])], axis=1
    ).astype(jnp.float32)
    k = jnp.concatenate(k_fine + k_coarse, axis=0)
    v = jnp.concatenate(v_fine + v_coarse, axis=0)
    v = jnp.concatenate([v, jnp.ones_like(v)], axis=1)
    n_fine = k.shape[0] - key_level.shape[1]

    def attend(queries, keys, values, allowed, h, rows, m_in, acc_in, m_out, acc_out):
        tile = rows.stop - rows.start
        s = dot_nt(queries[rows, h * HD : (h + 1) * HD], keys)
        if allowed is not None:
            s = jnp.where(allowed, s, LOW)
        top = jnp.max(s, axis=1, keepdims=True)
        if first:
            new = jnp.broadcast_to(top, (tile, HD))
        else:
            old = m_in[h, rows, :]
            new = jnp.maximum(old, top)
        p = jnp.exp2(s * EXPONENT - new[:, :1] * EXPONENT).astype(jnp.bfloat16)
        acc = dot_nn(p, values)
        if not first:
            acc = acc + acc_in[h, rows, :] * jnp.exp2((old - new) * EXPONENT)[:, :1]
        if not last:
            m_out[h, rows, :] = new
            acc_out[h, rows, :] = acc
            return None
        return (acc[:, :HD] / acc[:, HD:]).astype(jnp.bfloat16), new, acc[:, HD:]

    for is_coarse in (False, True):
        queries = cq_ref if is_coarse else q_ref
        pair = 2 if is_coarse else 0
        m_in, acc_in = (None, None) if first else state[pair : pair + 2]
        m_out, acc_out = (None, None) if last else refs[pair : pair + 2]
        half = queries.shape[0] // 2
        tile = min(TILE, half)
        lane = lax.broadcasted_iota(jnp.int32, (tile, HD), 1)
        begin, end = (part * half, (part + 1) * half) if last else (0, 2 * half)
        for start in range(begin, end, tile):
            rows = slice(start, start + tile)
            if is_coarse:
                allowed = key_level <= level_ref[rows, :1]
                keys, values = k[n_fine:], v[n_fine:]
            else:
                allowed, keys, values = None, k, v
            top = jnp.zeros((tile, HD), jnp.float32)
            total = jnp.ones((tile, HD), jnp.float32)
            for h in range(heads):
                done = attend(queries, keys, values, allowed, h, rows, m_in, acc_in, m_out, acc_out)
                if last:
                    place(refs, is_coarse, start - begin, q_ref.shape[0] // 4, h, done[0])
                    top = jnp.where(lane // 3 == h, done[1], top)
                    total = jnp.where(lane // 3 == h, done[2], total)
            if last:
                stats = in_three(top * EXPONENT + jnp.log(total) * math.log2(math.e), lane % 3)
                place(refs, is_coarse, start - begin, q_ref.shape[0] // 4, heads, stats)


def place(outs, is_coarse, begin, n_fine, h, value):
    n = outs[0].shape[0] - n_fine if is_coarse else n_fine
    length = min(n, value.shape[0])
    for i in range(value.shape[0] // length):
        row = begin + i * length
        start = row % n + (n_fine if is_coarse else 0)
        outs[row // n][start : start + length, h * HD : (h + 1) * HD] = value[
            i * length : (i + 1) * length
        ]


def fold(q, cq, level, blocks, state, part, fine, coarse):
    heads = q.shape[1] // HD
    first = state is None
    ins = (q, cq, level, *blocks, *(() if first else state))
    last = part is not None
    if last:
        quarter = (q.shape[0] + cq.shape[0]) // 4
        out = (jax.ShapeDtypeStruct((quarter, q.shape[1] + HD), jnp.bfloat16),) * 2
    else:
        out = tuple(
            jax.ShapeDtypeStruct((heads, rows, width), jnp.float32)
            for rows in (q.shape[0], cq.shape[0])
            for width in (HD, 2 * HD)
        )
    work = heads * sum(b.shape[0] for b in blocks) * (q.shape[0] * (fine + coarse) + cq.shape[0] * coarse)
    aliases = {} if first or last else {len(ins) - 4 + i: i for i in range(4)}
    return pl.pallas_call(
        functools.partial(fold_kernel, len(blocks), fine, coarse, first, part),
        out_shape=out,
        in_specs=[whole(a.shape) for a in ins],
        out_specs=tuple(whole(o.shape) for o in out),
        input_output_aliases=aliases,
        compiler_params=pltpu.CompilerParams(vmem_limit_bytes=GRANT),
        cost_estimate=pl.CostEstimate(
            flops=(work if last else 8 * work * HD), bytes_accessed=q.size, transcendentals=0
        ),
        name="fold",
    )(*ins)


def project_kernel(n_fine, n_blocks, place_ref, keep, near, cross, far, w, w_mine, w_other, *refs):
    outs, a_ref = refs[:-1], refs[-1]
    heads = keep.shape[1] // HD - 1
    rows = keep.shape[0]
    width = heads * HD
    half = width // 2

    @pl.when(pl.program_id(0) == 0)
    def _():
        swap = jnp.broadcast_to(place_ref[0], (1, 1)) == 1
        for g, (one, two) in enumerate(((keep, near), (cross, far))):
            merged = []
            for h in range(heads):
                stat = []
                for ref in (one, two):
                    s = ref[:, width:].astype(jnp.float32)
                    stat.append(s[:, 3 * h : 3 * h + 1] + s[:, 3 * h + 1 : 3 * h + 2] + s[:, 3 * h + 2 : 3 * h + 3])
                top = jnp.maximum(stat[0], stat[1])
                w0, w1 = jnp.exp2(stat[0] - top), jnp.exp2(stat[1] - top)
                cols = slice(h * HD, (h + 1) * HD)
                total = one[:, cols].astype(jnp.float32) * w0 + two[:, cols].astype(jnp.float32) * w1
                merged.append((total / (w0 + w1)).astype(jnp.bfloat16))
            merged = jnp.concatenate(merged, axis=1)
            if g == 1:
                lower, upper = merged[:, :half], merged[:, half:]
                merged = jnp.concatenate(
                    [jnp.where(swap, upper, lower), jnp.where(swap, lower, upper)], axis=1
                )
            n_coarse = rows - n_fine
            f, c = n_fine // n_blocks, n_coarse // n_blocks
            for b in range(n_blocks):
                at = jnp.bitwise_xor(place_ref[1], b) * (f + c)
                cols = slice(g * width, (g + 1) * width)
                a_ref[pl.ds(pl.multiple_of(at, c), f), cols] = merged[b * f : (b + 1) * f]
                a_ref[pl.ds(pl.multiple_of(at + f, c), c), cols] = merged[
                    n_fine + b * c : n_fine + (b + 1) * c
                ]

    share = (
        dot_nn(a_ref[:, :width], w[...])
        + dot_nn(a_ref[:, width : width + half], w_mine[...])
        + dot_nn(a_ref[:, width + half :], w_other[...])
    ).astype(jnp.bfloat16)
    size = rows // n_blocks
    for i, out in enumerate(outs):
        out[...] = share[i * size : (i + 1) * size]


def project(places, parts, weights, n_fine, n_blocks):
    rows = parts[0].shape[0]
    columns = weights[0].shape[1]
    tile = math.gcd(columns, 1024)
    depth = sum(w.shape[0] for w in weights)
    return pl.pallas_call(
        functools.partial(project_kernel, n_fine, n_blocks),
        grid=(columns // tile,),
        out_shape=(jax.ShapeDtypeStruct((rows // n_blocks, columns), jnp.bfloat16),) * n_blocks,
        in_specs=[pl.BlockSpec(memory_space=pltpu.SMEM)]
        + [whole(p.shape) for p in parts]
        + [pl.BlockSpec((w.shape[0], tile), lambda j: (0, j)) for w in weights],
        out_specs=(pl.BlockSpec((rows // n_blocks, tile), lambda j: (0, j)),) * n_blocks,
        scratch_shapes=[pltpu.VMEM((rows, depth), jnp.bfloat16)],
        compiler_params=pltpu.CompilerParams(vmem_limit_bytes=GRANT),
        cost_estimate=pl.CostEstimate(
            flops=2 * rows * depth * columns, bytes_accessed=2 * depth * columns, transcendentals=0
        ),
        name="project",
    )(places, *parts, *weights)


def crossed(x, axes):
    n = 2 ** len(axes)
    return lax.ppermute(x, axes, [(i, n - 1 - i) for i in range(n)])


def along_z(x, hops):
    n = lax.axis_size("z")
    pairs = []
    for z in range(n):
        pairs.append((2 * z, 2 * ((z + hops) % n)))
        pairs.append((2 * z + 1, 2 * ((z - hops) % n) + 1))
    return lax.ppermute(x, ("z", "c"), pairs)


def arrange_kernel(n_yh, n_xp, n_xl, xp_ref, fine_mine, fine_theirs, coarse_mine, coarse_theirs, q, cq, level):
    n = n_yh * n_xl
    width = q.shape[1]
    for whose, (fine, coarse) in enumerate(((fine_mine, coarse_mine), (fine_theirs, coarse_theirs))):
        for part in range(2):
            xp = xp_ref[0] if part == 0 else 1 - xp_ref[0]
            for i in range(n):
                block = (i // n_xl * n_xp + xp) * n_xl + i % n_xl
                at = (whose * 2 + part) * n + i
                size = fine.shape[0] // (2 * n)
                start = pl.multiple_of(block * size, size)
                q[at * size : (at + 1) * size, :] = fine[pl.ds(start, size), :]
                size = coarse.shape[0] // (2 * n)
                start = pl.multiple_of(block * size, size)
                rows = coarse[pl.ds(start, size), :]
                cq[at * size : (at + 1) * size, :] = rows[:, :width]
                level[at * size : (at + 1) * size, :] = rows[:, width:].astype(jnp.float32)


def arranged(xp, arrays):
    fine, coarse = arrays[0], arrays[2]
    width = fine.shape[1]
    out = (
        jax.ShapeDtypeStruct((2 * fine.shape[0], width), jnp.bfloat16),
        jax.ShapeDtypeStruct((2 * coarse.shape[0], width), jnp.bfloat16),
        jax.ShapeDtypeStruct((2 * coarse.shape[0], HD), jnp.float32),
    )
    return pl.pallas_call(
        functools.partial(arrange_kernel, *(lax.axis_size(a) for a in HEAD)),
        out_shape=out,
        in_specs=[pl.BlockSpec(memory_space=pltpu.SMEM)] + [whole(a.shape) for a in arrays],
        out_specs=tuple(whole(o.shape) for o in out),
        compiler_params=pltpu.CompilerParams(vmem_limit_bytes=GRANT),
        cost_estimate=pl.CostEstimate(
            flops=0, bytes_accessed=sum(4 * a.size for a in arrays), transcendentals=0
        ),
        name="arrange",
    )(xp, *arrays)


def after_kernel(*refs):
    pltpu.touch(refs[-1])


def after(x, before):
    return pl.pallas_call(
        after_kernel,
        out_shape=jax.ShapeDtypeStruct(x.shape, x.dtype),
        in_specs=[pl.BlockSpec(memory_space=pl.ANY)] * (1 + len(before)),
        out_specs=pl.BlockSpec(memory_space=pl.ANY),
        input_output_aliases={0: 0},
        compiler_params=pltpu.CompilerParams(vmem_limit_bytes=1 << 20),
        name="after",
    )(x, *before)


def per_device(fine_query, fine_memory, coarse_query, coarse_memory, coarse_scale, out_weight):
    fine, coarse = fine_query.shape[0], coarse_query.shape[0]
    width = fine_query.shape[1]
    levels = coarse_scale.astype(jnp.bfloat16)
    level_rows = jnp.broadcast_to(levels[None, :], (PAD, HD))
    piece = jnp.concatenate(
        [fine_memory.reshape(-1, HD), coarse_memory.reshape(-1, HD), level_rows], axis=0
    )
    coarse_mine = jnp.concatenate(
        [coarse_query, jnp.broadcast_to(levels[:, None], (coarse, HD))], axis=1
    )
    fine_theirs = crossed(fine_query, ("yl",))
    coarse_theirs = crossed(coarse_mine, ("yl",))

    chip = jnp.stack([piece, crossed(piece, ("c",))])
    one, two = along_z(chip, 1), along_z(chip, 2)

    core = lax.axis_index("c")
    depth = out_weight.shape[0] // 2
    weight_mine = crossed(lax.dynamic_slice_in_dim(out_weight, core * depth, depth, 0), ("xp",))

    q, cq, query_level = arranged(
        lax.axis_index("xp").reshape(1), (fine_query, fine_theirs, coarse_mine, coarse_theirs)
    )

    def folded(blocks, state, part):
        return fold(q, cq, query_level, blocks, state, part, fine, coarse)

    def with_twins(arrivals):
        return [b for x in arrivals for b in (x, crossed(x, ("c",)))]

    state = folded([chip], None, None)
    state, one, two = lax.optimization_barrier((state, one, two))
    three, four = along_z(one, 2), along_z(two[: two.shape[0] // 2], 2)
    state = folded(with_twins((one, two)), state, None)
    state, three, four = lax.optimization_barrier((state, three, four))
    blocks = with_twins((three, four))
    to_yl, to_both = folded(blocks, state, 1)
    near, far = crossed(to_yl, ("yl",)), crossed(to_both, ("yl", "xp"))
    keep, to_xp = folded(blocks, state, 0)
    across = crossed(to_xp, ("xp",))
    weight_mine = after(weight_mine, (near, far, across))
    weight_other = crossed(weight_mine, ("c",))
    shares = project(
        jnp.stack([core, lax.axis_index((HEAD[0], HEAD[2]))]),
        (keep, near, across, far),
        (out_weight, weight_mine, weight_other),
        fine // 2,
        4,
    )
    got = [shares[0]]
    for share, axes in zip(shares[1:], ((HEAD[2],), (HEAD[0],), (HEAD[0], HEAD[2]))):
        got.append(crossed(share, axes))
    split = got[0].shape[0] * fine // (fine + coarse)

    def total(rows):
        return sum(g[rows].astype(jnp.float32) for g in got).astype(jnp.bfloat16)

    return total(slice(0, split)), total(slice(split, None))


def solution(mesh):
    torus = Mesh(
        mesh.devices.reshape(2, 8, 2, 2, 2, 2), ("yl", "z", "c", "yh", "xp", "xl")
    )
    placed = (
        P(CTX, HEAD),
        P(None, CTX, HEAD),
        P(CTX, HEAD),
        P(None, CTX, HEAD),
        P(CTX),
        P(HEAD, None),
    )
    return jax.shard_map(
        per_device,
        mesh=torus,
        in_specs=placed,
        out_specs=(P(CTX + HEAD, None), P(CTX + HEAD, None)),
        check_vma=False,
    )
```

```python
import functools
import math

import jax
import jax.numpy as jnp
from jax import lax
from jax.experimental import pallas as pl
from jax.experimental.pallas import tpu as pltpu
from jax.sharding import Mesh
from jax.sharding import PartitionSpec as P

HD = 128
PAD = 16
CTX = ("yl", "z", "c")
HEAD = ("yh", "xp", "xl")
LOW = -1e30
EXPONENT = HD**-0.5 * math.log2(math.e)
NT = (((1,), (1,)), ((), ()))
NN = (((1,), (0,)), ((), ()))
GRANT = 24 << 20
TILE = 256


def dot_nt(a, b):
    return lax.dot_general(a, b, NT, preferred_element_type=jnp.float32)


def dot_nn(a, b):
    return lax.dot_general(a, b, NN, preferred_element_type=jnp.float32)


def whole(shape):
    return pl.BlockSpec(shape, lambda *_: (0,) * len(shape))


def rows_of(ref, start, length):
    return ref[:, start : start + length, :].reshape(-1, HD)


def in_three(x, which):
    result = jnp.zeros_like(x)
    for i in range(3):
        part = x.astype(jnp.bfloat16).astype(jnp.float32)
        result = jnp.where(which == i, part, result)
        x = x - part
    return result.astype(jnp.bfloat16)


def fold_kernel(n_blocks, fine, coarse, first, part, q_ref, cq_ref, level_ref, *refs):
    last = part is not None
    blocks, refs = refs[:n_blocks], refs[n_blocks:]
    if not first:
        state, refs = refs[:4], refs[4:]
    heads = q_ref.shape[1] // HD
    at = 2 * fine
    k_fine = [rows_of(b, 0, fine) for b in blocks]
    v_fine = [rows_of(b, fine, fine) for b in blocks]
    k_coarse = [rows_of(b, at, coarse) for b in blocks]
    v_coarse = [rows_of(b, at + coarse, coarse) for b in blocks]
    at = at + 2 * coarse
    key_level = jnp.concatenate(
        [b[i, at : at + 1, :] for b in blocks for i in range(b.shape[0])], axis=1
    ).astype(jnp.float32)
    k = jnp.concatenate(k_fine + k_coarse, axis=0)
    v = jnp.concatenate(v_fine + v_coarse, axis=0)
    v = jnp.concatenate([v, jnp.ones_like(v)], axis=1)
    n_fine = k.shape[0] - key_level.shape[1]

    def attend(queries, keys, values, allowed, h, rows, m_in, acc_in, m_out, acc_out):
        tile = rows.stop - rows.start
        s = dot_nt(queries[rows, h * HD : (h + 1) * HD], keys)
        if allowed is not None:
            s = jnp.where(allowed, s, LOW)
        top = jnp.max(s, axis=1, keepdims=True)
        if first:
            new = jnp.broadcast_to(top, (tile, HD))
        else:
            old = m_in[h, rows, :]
            new = jnp.maximum(old, top)
        p = jnp.exp2(s * EXPONENT - new[:, :1] * EXPONENT).astype(jnp.bfloat16)
        acc = dot_nn(p, values)
        if not first:
            acc = acc + acc_in[h, rows, :] * jnp.exp2((old - new) * EXPONENT)[:, :1]
        if not last:
            m_out[h, rows, :] = new
            acc_out[h, rows, :] = acc
            return None
        return (acc[:, :HD] / acc[:, HD:]).astype(jnp.bfloat16), new, acc[:, HD:]

    for is_coarse in (False, True):
        queries = cq_ref if is_coarse else q_ref
        pair = 2 if is_coarse else 0
        m_in, acc_in = (None, None) if first else state[pair : pair + 2]
        m_out, acc_out = (None, None) if last else refs[pair : pair + 2]
        half = queries.shape[0] // 2
        tile = min(TILE, half)
        lane = lax.broadcasted_iota(jnp.int32, (tile, HD), 1)
        begin, end = (part * half, (part + 1) * half) if last else (0, 2 * half)
        for start in range(begin, end, tile):
            rows = slice(start, start + tile)
            if is_coarse:
                allowed = key_level <= level_ref[rows, :1]
                keys, values = k[n_fine:], v[n_fine:]
            else:
                allowed, keys, values = None, k, v
            top = jnp.zeros((tile, HD), jnp.float32)
            total = jnp.ones((tile, HD), jnp.float32)
            for h in range(heads):
                done = attend(queries, keys, values, allowed, h, rows, m_in, acc_in, m_out, acc_out)
                if last:
                    place(refs, is_coarse, start - begin, q_ref.shape[0] // 4, h, done[0])
                    top = jnp.where(lane // 3 == h, done[1], top)
                    total = jnp.where(lane // 3 == h, done[2], total)
            if last:
                stats = in_three(top * EXPONENT + jnp.log(total) * math.log2(math.e), lane % 3)
                place(refs, is_coarse, start - begin, q_ref.shape[0] // 4, heads, stats)


def place(outs, is_coarse, begin, n_fine, h, value):
    n = outs[0].shape[0] - n_fine if is_coarse else n_fine
    length = min(n, value.shape[0])
    for i in range(value.shape[0] // length):
        row = begin + i * length
        start = row % n + (n_fine if is_coarse else 0)
        outs[row // n][start : start + length, h * HD : (h + 1) * HD] = value[
            i * length : (i + 1) * length
        ]


def fold(q, cq, level, blocks, state, part, fine, coarse):
    heads = q.shape[1] // HD
    first = state is None
    ins = (q, cq, level, *blocks, *(() if first else state))
    last = part is not None
    if last:
        quarter = (q.shape[0] + cq.shape[0]) // 4
        out = (jax.ShapeDtypeStruct((quarter, q.shape[1] + HD), jnp.bfloat16),) * 2
    else:
        out = tuple(
            jax.ShapeDtypeStruct((heads, rows, width), jnp.float32)
            for rows in (q.shape[0], cq.shape[0])
            for width in (HD, 2 * HD)
        )
    work = heads * sum(b.shape[0] for b in blocks) * (q.shape[0] * (fine + coarse) + cq.shape[0] * coarse)
    aliases = {} if first or last else {len(ins) - 4 + i: i for i in range(4)}
    return pl.pallas_call(
        functools.partial(fold_kernel, len(blocks), fine, coarse, first, part),
        out_shape=out,
        in_specs=[whole(a.shape) for a in ins],
        out_specs=tuple(whole(o.shape) for o in out),
        input_output_aliases=aliases,
        compiler_params=pltpu.CompilerParams(vmem_limit_bytes=GRANT),
        cost_estimate=pl.CostEstimate(
            flops=(work if last else 8 * work * HD), bytes_accessed=q.size, transcendentals=0
        ),
        name="fold",
    )(*ins)


def project_kernel(n_fine, n_blocks, place_ref, keep, near, cross, far, w, w_mine, share_ref, rest_ref, a_ref):
    heads = keep.shape[1] // HD - 1
    rows = keep.shape[0]
    width = heads * HD
    half = width // 2

    @pl.when(pl.program_id(0) == 0)
    def _():
        swap = jnp.broadcast_to(place_ref[0], (1, 1)) == 1
        for g, (one, two) in enumerate(((keep, near), (cross, far))):
            merged = []
            for h in range(heads):
                stat = []
                for ref in (one, two):
                    s = ref[:, width:].astype(jnp.float32)
                    stat.append(s[:, 3 * h : 3 * h + 1] + s[:, 3 * h + 1 : 3 * h + 2] + s[:, 3 * h + 2 : 3 * h + 3])
                top = jnp.maximum(stat[0], stat[1])
                w0, w1 = jnp.exp2(stat[0] - top), jnp.exp2(stat[1] - top)
                cols = slice(h * HD, (h + 1) * HD)
                total = one[:, cols].astype(jnp.float32) * w0 + two[:, cols].astype(jnp.float32) * w1
                merged.append((total / (w0 + w1)).astype(jnp.bfloat16))
            merged = jnp.concatenate(merged, axis=1)
            if g == 1:
                lower, upper = merged[:, :half], merged[:, half:]
                merged = jnp.concatenate(
                    [jnp.where(swap, upper, lower), jnp.where(swap, lower, upper)], axis=1
                )
            n_coarse = rows - n_fine
            f, c = n_fine // n_blocks, n_coarse // n_blocks
            for b in range(n_blocks):
                at = jnp.bitwise_xor(place_ref[1], b) * (f + c)
                cols = slice(g * width, (g + 1) * width)
                a_ref[pl.ds(pl.multiple_of(at, c), f), cols] = merged[b * f : (b + 1) * f]
                a_ref[pl.ds(pl.multiple_of(at + f, c), c), cols] = merged[
                    n_fine + b * c : n_fine + (b + 1) * c
                ]

        rest_ref[...] = a_ref[:, width + half :]

    share_ref[...] = dot_nn(a_ref[:, :width], w[...]) + dot_nn(
        a_ref[:, width : width + half], w_mine[...]
    )


def project(places, parts, weights, n_fine, n_blocks):
    rows = parts[0].shape[0]
    columns = weights[0].shape[1]
    tile = math.gcd(columns, 1024)
    half = weights[1].shape[0]
    depth = weights[0].shape[0] + 2 * half
    return pl.pallas_call(
        functools.partial(project_kernel, n_fine, n_blocks),
        grid=(columns // tile,),
        out_shape=(
            jax.ShapeDtypeStruct((rows, columns), jnp.float32),
            jax.ShapeDtypeStruct((rows, half), jnp.bfloat16),
        ),
        in_specs=[pl.BlockSpec(memory_space=pltpu.SMEM)]
        + [whole(p.shape) for p in parts]
        + [pl.BlockSpec((w.shape[0], tile), lambda j: (0, j)) for w in weights],
        out_specs=(pl.BlockSpec((rows, tile), lambda j: (0, j)), whole((rows, half))),
        scratch_shapes=[pltpu.VMEM((rows, depth), jnp.bfloat16)],
        compiler_params=pltpu.CompilerParams(vmem_limit_bytes=GRANT),
        cost_estimate=pl.CostEstimate(
            flops=2 * rows * (depth - half) * columns, bytes_accessed=2 * depth * columns, transcendentals=0
        ),
        name="project",
    )(places, *parts, *weights)


def complete_kernel(share_ref, rest_ref, w, *outs):
    share = (share_ref[...] + dot_nn(rest_ref[...], w[...])).astype(jnp.bfloat16)
    size = share.shape[0] // len(outs)
    for i, out in enumerate(outs):
        out[...] = share[i * size : (i + 1) * size]


def completed(share, rest, weight, n_blocks):
    rows, columns = share.shape
    tile = math.gcd(columns, 1024)
    return pl.pallas_call(
        complete_kernel,
        grid=(columns // tile,),
        out_shape=(jax.ShapeDtypeStruct((rows // n_blocks, columns), jnp.bfloat16),) * n_blocks,
        in_specs=[
            pl.BlockSpec((rows, tile), lambda j: (0, j)),
            whole(rest.shape),
            pl.BlockSpec((weight.shape[0], tile), lambda j: (0, j)),
        ],
        out_specs=(pl.BlockSpec((rows // n_blocks, tile), lambda j: (0, j)),) * n_blocks,
        compiler_params=pltpu.CompilerParams(vmem_limit_bytes=GRANT),
        cost_estimate=pl.CostEstimate(
            flops=2 * rows * weight.size, bytes_accessed=4 * share.size, transcendentals=0
        ),
        name="complete",
    )(share, rest, weight)


def crossed(x, axes):
    n = 2 ** len(axes)
    return lax.ppermute(x, axes, [(i, n - 1 - i) for i in range(n)])


def along_z(x, hops):
    n = lax.axis_size("z")
    pairs = []
    for z in range(n):
        pairs.append((2 * z, 2 * ((z + hops) % n)))
        pairs.append((2 * z + 1, 2 * ((z - hops) % n) + 1))
    return lax.ppermute(x, ("z", "c"), pairs)


def arrange_kernel(n_yh, n_xp, n_xl, xp_ref, fine_mine, fine_theirs, coarse_mine, coarse_theirs, q, cq, level):
    n = n_yh * n_xl
    width = q.shape[1]
    for whose, (fine, coarse) in enumerate(((fine_mine, coarse_mine), (fine_theirs, coarse_theirs))):
        for part in range(2):
            xp = xp_ref[0] if part == 0 else 1 - xp_ref[0]
            for i in range(n):
                block = (i // n_xl * n_xp + xp) * n_xl + i % n_xl
                at = (whose * 2 + part) * n + i
                size = fine.shape[0] // (2 * n)
                start = pl.multiple_of(block * size, size)
                q[at * size : (at + 1) * size, :] = fine[pl.ds(start, size), :]
                size = coarse.shape[0] // (2 * n)
                start = pl.multiple_of(block * size, size)
                rows = coarse[pl.ds(start, size), :]
                cq[at * size : (at + 1) * size, :] = rows[:, :width]
                level[at * size : (at + 1) * size, :] = rows[:, width:].astype(jnp.float32)


def arranged(xp, arrays):
    fine, coarse = arrays[0], arrays[2]
    width = fine.shape[1]
    out = (
        jax.ShapeDtypeStruct((2 * fine.shape[0], width), jnp.bfloat16),
        jax.ShapeDtypeStruct((2 * coarse.shape[0], width), jnp.bfloat16),
        jax.ShapeDtypeStruct((2 * coarse.shape[0], HD), jnp.float32),
    )
    return pl.pallas_call(
        functools.partial(arrange_kernel, *(lax.axis_size(a) for a in HEAD)),
        out_shape=out,
        in_specs=[pl.BlockSpec(memory_space=pltpu.SMEM)] + [whole(a.shape) for a in arrays],
        out_specs=tuple(whole(o.shape) for o in out),
        compiler_params=pltpu.CompilerParams(vmem_limit_bytes=GRANT),
        cost_estimate=pl.CostEstimate(
            flops=0, bytes_accessed=sum(4 * a.size for a in arrays), transcendentals=0
        ),
        name="arrange",
    )(xp, *arrays)


def after_kernel(*refs):
    pltpu.touch(refs[-1])


def after(x, before):
    return pl.pallas_call(
        after_kernel,
        out_shape=jax.ShapeDtypeStruct(x.shape, x.dtype),
        in_specs=[pl.BlockSpec(memory_space=pl.ANY)] * (1 + len(before)),
        out_specs=pl.BlockSpec(memory_space=pl.ANY),
        input_output_aliases={0: 0},
        compiler_params=pltpu.CompilerParams(vmem_limit_bytes=1 << 20),
        name="after",
    )(x, *before)


def per_device(fine_query, fine_memory, coarse_query, coarse_memory, coarse_scale, out_weight):
    fine, coarse = fine_query.shape[0], coarse_query.shape[0]
    width = fine_query.shape[1]
    levels = coarse_scale.astype(jnp.bfloat16)
    level_rows = jnp.broadcast_to(levels[None, :], (PAD, HD))
    piece = jnp.concatenate(
        [fine_memory.reshape(-1, HD), coarse_memory.reshape(-1, HD), level_rows], axis=0
    )
    coarse_mine = jnp.concatenate(
        [coarse_query, jnp.broadcast_to(levels[:, None], (coarse, HD))], axis=1
    )
    fine_theirs = crossed(fine_query, ("yl",))
    coarse_theirs = crossed(coarse_mine, ("yl",))

    chip = jnp.stack([piece, crossed(piece, ("c",))])
    one, two = along_z(chip, 1), along_z(chip, 2)

    core = lax.axis_index("c")
    depth = out_weight.shape[0] // 2
    weight_mine = crossed(lax.dynamic_slice_in_dim(out_weight, core * depth, depth, 0), ("xp",))

    q, cq, query_level = arranged(
        lax.axis_index("xp").reshape(1), (fine_query, fine_theirs, coarse_mine, coarse_theirs)
    )

    def folded(blocks, state, part):
        return fold(q, cq, query_level, blocks, state, part, fine, coarse)

    def with_twins(arrivals):
        return [b for x in arrivals for b in (x, crossed(x, ("c",)))]

    state = folded([chip], None, None)
    state, one, two = lax.optimization_barrier((state, one, two))
    three, four = along_z(one, 2), along_z(two[: two.shape[0] // 2], 2)
    state = folded(with_twins((one, two)), state, None)
    state, three, four = lax.optimization_barrier((state, three, four))
    blocks = with_twins((three, four))
    to_yl, to_both = folded(blocks, state, 1)
    near, far = crossed(to_yl, ("yl",)), crossed(to_both, ("yl", "xp"))
    keep, to_xp = folded(blocks, state, 0)
    across = crossed(to_xp, ("xp",))
    weight_mine = after(weight_mine, (near, far, across))
    weight_other = crossed(weight_mine, ("c",))
    share, rest = project(
        jnp.stack([core, lax.axis_index((HEAD[0], HEAD[2]))]),
        (keep, near, across, far),
        (out_weight, weight_mine),
        fine // 2,
        4,
    )
    shares = completed(share, rest, weight_other, 4)
    got = [shares[0]]
    for share, axes in zip(shares[1:], ((HEAD[2],), (HEAD[0],), (HEAD[0], HEAD[2]))):
        got.append(crossed(share, axes))
    split = got[0].shape[0] * fine // (fine + coarse)

    def total(rows):
        return sum(g[rows].astype(jnp.float32) for g in got).astype(jnp.bfloat16)

    return total(slice(0, split)), total(slice(split, None))


def solution(mesh):
    torus = Mesh(
        mesh.devices.reshape(2, 8, 2, 2, 2, 2), ("yl", "z", "c", "yh", "xp", "xl")
    )
    placed = (
        P(CTX, HEAD),
        P(None, CTX, HEAD),
        P(CTX, HEAD),
        P(None, CTX, HEAD),
        P(CTX),
        P(HEAD, None),
    )
    return jax.shard_map(
        per_device,
        mesh=torus,
        in_specs=placed,
        out_specs=(P(CTX + HEAD, None), P(CTX + HEAD, None)),
        check_vma=False,
    )
```

```python
import functools
import math

import jax
import jax.numpy as jnp
from jax import lax
from jax.experimental import pallas as pl
from jax.experimental.pallas import tpu as pltpu
from jax.sharding import Mesh
from jax.sharding import PartitionSpec as P

HD = 128
PAD = 16
CTX = ("yl", "z", "c")
HEAD = ("yh", "xp", "xl")
LOW = -1e30
EXPONENT = HD**-0.5 * math.log2(math.e)
NT = (((1,), (1,)), ((), ()))
NN = (((1,), (0,)), ((), ()))
GRANT = 24 << 20
TILE = 256


def dot_nt(a, b):
    return lax.dot_general(a, b, NT, preferred_element_type=jnp.float32)


def dot_nn(a, b):
    return lax.dot_general(a, b, NN, preferred_element_type=jnp.float32)


def whole(shape):
    return pl.BlockSpec(shape, lambda *_: (0,) * len(shape))


def rows_of(ref, start, length):
    return ref[:, start : start + length, :].reshape(-1, HD)


def in_three(x, which):
    result = jnp.zeros_like(x)
    for i in range(3):
        part = x.astype(jnp.bfloat16).astype(jnp.float32)
        result = jnp.where(which == i, part, result)
        x = x - part
    return result.astype(jnp.bfloat16)


def fold_kernel(n_blocks, fine, coarse, first, part, q_ref, cq_ref, level_ref, *refs):
    last = part is not None
    blocks, refs = refs[:n_blocks], refs[n_blocks:]
    if not first:
        state, refs = refs[:4], refs[4:]
    heads = q_ref.shape[1] // HD
    at = 2 * fine
    k_fine = [rows_of(b, 0, fine) for b in blocks]
    v_fine = [rows_of(b, fine, fine) for b in blocks]
    k_coarse = [rows_of(b, at, coarse) for b in blocks]
    v_coarse = [rows_of(b, at + coarse, coarse) for b in blocks]
    at = at + 2 * coarse
    key_level = jnp.concatenate(
        [b[i, at : at + 1, :] for b in blocks for i in range(b.shape[0])], axis=1
    ).astype(jnp.float32)
    k = jnp.concatenate(k_fine + k_coarse, axis=0)
    v = jnp.concatenate(v_fine + v_coarse, axis=0)
    v = jnp.concatenate([v, jnp.ones_like(v)], axis=1)
    n_fine = k.shape[0] - key_level.shape[1]

    def attend(queries, keys, values, allowed, h, rows, m_in, acc_in, m_out, acc_out):
        tile = rows.stop - rows.start
        s = dot_nt(queries[rows, h * HD : (h + 1) * HD], keys)
        if allowed is not None:
            s = jnp.where(allowed, s, LOW)
        top = jnp.max(s, axis=1, keepdims=True)
        if first:
            new = jnp.broadcast_to(top, (tile, HD))
        else:
            old = m_in[h, rows, :]
            new = jnp.maximum(old, top)
        p = jnp.exp2(s * EXPONENT - new[:, :1] * EXPONENT).astype(jnp.bfloat16)
        acc = dot_nn(p, values)
        if not first:
            acc = acc + acc_in[h, rows, :] * jnp.exp2((old - new) * EXPONENT)[:, :1]
        if not last:
            m_out[h, rows, :] = new
            acc_out[h, rows, :] = acc
            return None
        return (acc[:, :HD] / acc[:, HD:]).astype(jnp.bfloat16), new, acc[:, HD:]

    for is_coarse in (False, True):
        queries = cq_ref if is_coarse else q_ref
        pair = 2 if is_coarse else 0
        m_in, acc_in = (None, None) if first else state[pair : pair + 2]
        m_out, acc_out = (None, None) if last else refs[pair : pair + 2]
        half = queries.shape[0] // 2
        tile = min(TILE, half)
        lane = lax.broadcasted_iota(jnp.int32, (tile, HD), 1)
        begin, end = (part * half, (part + 1) * half) if last else (0, 2 * half)
        for start in range(begin, end, tile):
            rows = slice(start, start + tile)
            if is_coarse:
                allowed = key_level <= level_ref[rows, :1]
                keys, values = k[n_fine:], v[n_fine:]
            else:
                allowed, keys, values = None, k, v
            top = jnp.zeros((tile, HD), jnp.float32)
            total = jnp.ones((tile, HD), jnp.float32)
            for h in range(heads):
                done = attend(queries, keys, values, allowed, h, rows, m_in, acc_in, m_out, acc_out)
                if last:
                    place(refs, is_coarse, start - begin, q_ref.shape[0] // 4, h, done[0])
                    top = jnp.where(lane // 3 == h, done[1], top)
                    total = jnp.where(lane // 3 == h, done[2], total)
            if last:
                stats = in_three(top * EXPONENT + jnp.log(total) * math.log2(math.e), lane % 3)
                place(refs, is_coarse, start - begin, q_ref.shape[0] // 4, heads, stats)


def place(outs, is_coarse, begin, n_fine, h, value):
    n = outs[0].shape[0] - n_fine if is_coarse else n_fine
    length = min(n, value.shape[0])
    for i in range(value.shape[0] // length):
        row = begin + i * length
        start = row % n + (n_fine if is_coarse else 0)
        outs[row // n][start : start + length, h * HD : (h + 1) * HD] = value[
            i * length : (i + 1) * length
        ]


def fold(q, cq, level, blocks, state, part, fine, coarse):
    heads = q.shape[1] // HD
    first = state is None
    ins = (q, cq, level, *blocks, *(() if first else state))
    last = part is not None
    if last:
        quarter = (q.shape[0] + cq.shape[0]) // 4
        out = (jax.ShapeDtypeStruct((quarter, q.shape[1] + HD), jnp.bfloat16),) * 2
    else:
        out = tuple(
            jax.ShapeDtypeStruct((heads, rows, width), jnp.float32)
            for rows in (q.shape[0], cq.shape[0])
            for width in (HD, 2 * HD)
        )
    work = heads * sum(b.shape[0] for b in blocks) * (q.shape[0] * (fine + coarse) + cq.shape[0] * coarse)
    aliases = {} if first or last else {len(ins) - 4 + i: i for i in range(4)}
    return pl.pallas_call(
        functools.partial(fold_kernel, len(blocks), fine, coarse, first, part),
        out_shape=out,
        in_specs=[whole(a.shape) for a in ins],
        out_specs=tuple(whole(o.shape) for o in out),
        input_output_aliases=aliases,
        compiler_params=pltpu.CompilerParams(vmem_limit_bytes=GRANT),
        cost_estimate=pl.CostEstimate(
            flops=(work if last else 8 * work * HD), bytes_accessed=q.size, transcendentals=0
        ),
        name="fold",
    )(*ins)


def tiles_of(columns):
    tile = math.gcd(columns, 1024)
    return [slice(start, start + tile) for start in range(0, columns, tile)]


def project_kernel(n_fine, n_blocks, place_ref, keep, near, cross, far, w, w_mine, share_ref, rest_ref, a_ref):
    heads = keep.shape[1] // HD - 1
    rows = keep.shape[0]
    width = heads * HD
    half = width // 2

    swap = jnp.broadcast_to(place_ref[0], (1, 1)) == 1
    for g, (one, two) in enumerate(((keep, near), (cross, far))):
        merged = []
        for h in range(heads):
            stat = []
            for ref in (one, two):
                s = ref[:, width:].astype(jnp.float32)
                stat.append(s[:, 3 * h : 3 * h + 1] + s[:, 3 * h + 1 : 3 * h + 2] + s[:, 3 * h + 2 : 3 * h + 3])
            top = jnp.maximum(stat[0], stat[1])
            w0, w1 = jnp.exp2(stat[0] - top), jnp.exp2(stat[1] - top)
            cols = slice(h * HD, (h + 1) * HD)
            total = one[:, cols].astype(jnp.float32) * w0 + two[:, cols].astype(jnp.float32) * w1
            merged.append((total / (w0 + w1)).astype(jnp.bfloat16))
        merged = jnp.concatenate(merged, axis=1)
        if g == 1:
            lower, upper = merged[:, :half], merged[:, half:]
            merged = jnp.concatenate(
                [jnp.where(swap, upper, lower), jnp.where(swap, lower, upper)], axis=1
            )
        n_coarse = rows - n_fine
        f, c = n_fine // n_blocks, n_coarse // n_blocks
        for b in range(n_blocks):
            at = jnp.bitwise_xor(place_ref[1], b) * (f + c)
            cols = slice(g * width, (g + 1) * width)
            a_ref[pl.ds(pl.multiple_of(at, c), f), cols] = merged[b * f : (b + 1) * f]
            a_ref[pl.ds(pl.multiple_of(at + f, c), c), cols] = merged[
                n_fine + b * c : n_fine + (b + 1) * c
            ]

    rest_ref[...] = a_ref[:, width + half :]

    for cols in tiles_of(w.shape[1]):
        share_ref[:, cols] = dot_nn(a_ref[:, :width], w[:, cols]) + dot_nn(
            a_ref[:, width : width + half], w_mine[:, cols]
        )


def project(places, parts, weights, n_fine, n_blocks):
    rows = parts[0].shape[0]
    columns = weights[0].shape[1]
    half = weights[1].shape[0]
    depth = weights[0].shape[0] + 2 * half
    return pl.pallas_call(
        functools.partial(project_kernel, n_fine, n_blocks),
        out_shape=(
            jax.ShapeDtypeStruct((rows, columns), jnp.float32),
            jax.ShapeDtypeStruct((rows, half), jnp.bfloat16),
        ),
        in_specs=[pl.BlockSpec(memory_space=pltpu.SMEM)]
        + [whole(p.shape) for p in parts]
        + [whole(w.shape) for w in weights],
        out_specs=(whole((rows, columns)), whole((rows, half))),
        scratch_shapes=[pltpu.VMEM((rows, depth), jnp.bfloat16)],
        compiler_params=pltpu.CompilerParams(vmem_limit_bytes=GRANT),
        cost_estimate=pl.CostEstimate(
            flops=2 * rows * (depth - half) * columns, bytes_accessed=2 * depth * columns, transcendentals=0
        ),
        name="project",
    )(places, *parts, *weights)


def complete_kernel(share_ref, rest_ref, w, *outs):
    for cols in tiles_of(w.shape[1]):
        share = (share_ref[:, cols] + dot_nn(rest_ref[...], w[:, cols])).astype(jnp.bfloat16)
        size = share.shape[0] // len(outs)
        for i, out in enumerate(outs):
            out[:, cols] = share[i * size : (i + 1) * size]


def completed(share, rest, weight, n_blocks):
    rows, columns = share.shape
    return pl.pallas_call(
        complete_kernel,
        out_shape=(jax.ShapeDtypeStruct((rows // n_blocks, columns), jnp.bfloat16),) * n_blocks,
        in_specs=[whole(a.shape) for a in (share, rest, weight)],
        out_specs=(whole((rows // n_blocks, columns)),) * n_blocks,
        compiler_params=pltpu.CompilerParams(vmem_limit_bytes=GRANT),
        cost_estimate=pl.CostEstimate(
            flops=2 * rows * weight.size, bytes_accessed=4 * share.size, transcendentals=0
        ),
        name="complete",
    )(share, rest, weight)


def crossed(x, axes):
    n = 2 ** len(axes)
    return lax.ppermute(x, axes, [(i, n - 1 - i) for i in range(n)])


def along_z(x, hops):
    n = lax.axis_size("z")
    pairs = []
    for z in range(n):
        pairs.append((2 * z, 2 * ((z + hops) % n)))
        pairs.append((2 * z + 1, 2 * ((z - hops) % n) + 1))
    return lax.ppermute(x, ("z", "c"), pairs)


def arrange_kernel(n_yh, n_xp, n_xl, xp_ref, fine_mine, fine_theirs, coarse_mine, coarse_theirs, q, cq, level):
    n = n_yh * n_xl
    width = q.shape[1]
    for whose, (fine, coarse) in enumerate(((fine_mine, coarse_mine), (fine_theirs, coarse_theirs))):
        for part in range(2):
            xp = xp_ref[0] if part == 0 else 1 - xp_ref[0]
            for i in range(n):
                block = (i // n_xl * n_xp + xp) * n_xl + i % n_xl
                at = (whose * 2 + part) * n + i
                size = fine.shape[0] // (2 * n)
                start = pl.multiple_of(block * size, size)
                q[at * size : (at + 1) * size, :] = fine[pl.ds(start, size), :]
                size = coarse.shape[0] // (2 * n)
                start = pl.multiple_of(block * size, size)
                rows = coarse[pl.ds(start, size), :]
                cq[at * size : (at + 1) * size, :] = rows[:, :width]
                level[at * size : (at + 1) * size, :] = rows[:, width:].astype(jnp.float32)


def arranged(xp, arrays):
    fine, coarse = arrays[0], arrays[2]
    width = fine.shape[1]
    out = (
        jax.ShapeDtypeStruct((2 * fine.shape[0], width), jnp.bfloat16),
        jax.ShapeDtypeStruct((2 * coarse.shape[0], width), jnp.bfloat16),
        jax.ShapeDtypeStruct((2 * coarse.shape[0], HD), jnp.float32),
    )
    return pl.pallas_call(
        functools.partial(arrange_kernel, *(lax.axis_size(a) for a in HEAD)),
        out_shape=out,
        in_specs=[pl.BlockSpec(memory_space=pltpu.SMEM)] + [whole(a.shape) for a in arrays],
        out_specs=tuple(whole(o.shape) for o in out),
        compiler_params=pltpu.CompilerParams(vmem_limit_bytes=GRANT),
        cost_estimate=pl.CostEstimate(
            flops=0, bytes_accessed=sum(4 * a.size for a in arrays), transcendentals=0
        ),
        name="arrange",
    )(xp, *arrays)


def after_kernel(*refs):
    pltpu.touch(refs[-1])


def after(x, before):
    return pl.pallas_call(
        after_kernel,
        out_shape=jax.ShapeDtypeStruct(x.shape, x.dtype),
        in_specs=[pl.BlockSpec(memory_space=pl.ANY)] * (1 + len(before)),
        out_specs=pl.BlockSpec(memory_space=pl.ANY),
        input_output_aliases={0: 0},
        compiler_params=pltpu.CompilerParams(vmem_limit_bytes=1 << 20),
        name="after",
    )(x, *before)


def per_device(fine_query, fine_memory, coarse_query, coarse_memory, coarse_scale, out_weight):
    fine, coarse = fine_query.shape[0], coarse_query.shape[0]
    width = fine_query.shape[1]
    levels = coarse_scale.astype(jnp.bfloat16)
    level_rows = jnp.broadcast_to(levels[None, :], (PAD, HD))
    piece = jnp.concatenate(
        [fine_memory.reshape(-1, HD), coarse_memory.reshape(-1, HD), level_rows], axis=0
    )
    coarse_mine = jnp.concatenate(
        [coarse_query, jnp.broadcast_to(levels[:, None], (coarse, HD))], axis=1
    )
    fine_theirs = crossed(fine_query, ("yl",))
    coarse_theirs = crossed(coarse_mine, ("yl",))

    chip = jnp.stack([piece, crossed(piece, ("c",))])
    one, two = along_z(chip, 1), along_z(chip, 2)

    core = lax.axis_index("c")
    depth = out_weight.shape[0] // 2
    weight_mine = crossed(lax.dynamic_slice_in_dim(out_weight, core * depth, depth, 0), ("xp",))

    q, cq, query_level = arranged(
        lax.axis_index("xp").reshape(1), (fine_query, fine_theirs, coarse_mine, coarse_theirs)
    )

    def folded(blocks, state, part):
        return fold(q, cq, query_level, blocks, state, part, fine, coarse)

    def with_twins(arrivals):
        return [b for x in arrivals for b in (x, crossed(x, ("c",)))]

    state = folded([chip], None, None)
    state, one, two = lax.optimization_barrier((state, one, two))
    three, four = along_z(one, 2), along_z(two[: two.shape[0] // 2], 2)
    state = folded(with_twins((one, two)), state, None)
    state, three, four = lax.optimization_barrier((state, three, four))
    blocks = with_twins((three, four))
    to_yl, to_both = folded(blocks, state, 1)
    near, far = crossed(to_yl, ("yl",)), crossed(to_both, ("yl", "xp"))
    keep, to_xp = folded(blocks, state, 0)
    across = crossed(to_xp, ("xp",))
    weight_mine = after(weight_mine, (near, far, across))
    weight_other = crossed(weight_mine, ("c",))
    share, rest = project(
        jnp.stack([core, lax.axis_index((HEAD[0], HEAD[2]))]),
        (keep, near, across, far),
        (out_weight, weight_mine),
        fine // 2,
        4,
    )
    shares = completed(share, rest, weight_other, 4)
    got = [shares[0]]
    for share, axes in zip(shares[1:], ((HEAD[2],), (HEAD[0],), (HEAD[0], HEAD[2]))):
        got.append(crossed(share, axes))
    split = got[0].shape[0] * fine // (fine + coarse)

    def total(rows):
        return sum(g[rows].astype(jnp.float32) for g in got).astype(jnp.bfloat16)

    return total(slice(0, split)), total(slice(split, None))


def solution(mesh):
    torus = Mesh(
        mesh.devices.reshape(2, 8, 2, 2, 2, 2), ("yl", "z", "c", "yh", "xp", "xl")
    )
    placed = (
        P(CTX, HEAD),
        P(None, CTX, HEAD),
        P(CTX, HEAD),
        P(None, CTX, HEAD),
        P(CTX),
        P(HEAD, None),
    )
    return jax.shard_map(
        per_device,
        mesh=torus,
        in_specs=placed,
        out_specs=(P(CTX + HEAD, None), P(CTX + HEAD, None)),
        check_vma=False,
    )
```
